128 devices in a mesh: tm: 2 (over x_lo), gz: 8 (over y, x_hi), view: 8 (over z, core).
Axes of the slice: x: 4 (x_hi: 2, x_lo: 2; x = x_hi * 2 + x_lo), y: 4, z: 4, core: 2. Of those that a mesh axis runs over, the one named last changes fastest.
Arguments:
- sinogram: bfloat16 [2, 16, 1024, 2560], P(None, 'view', ('tm', 'gz')), may hold values from 102 to 358
- projector: bfloat16 [16, 1024, 2560], P('view'), may hold values from 0.0099487305 to 1
- warm_volume: float32 [1024, 1024], P(('tm', 'gz')), may hold values from 0.2 to 2.5, as said below
- view_order: int32 [2], replicated, may hold values from 0 to 1, each once
Outputs:
- volumes: float32 [2, 1024, 1024], P(None, ('tm', 'gz'))
The draws below stay inside these ranges and needn't reach their ends.
Inputs may be any that keep to these rules, and one draw needn't show every extreme that they name: `view_order`: each local view number appears once. `warm_volume`: positive attenuation values.
All inputs are finite; a program needn't handle non-finite values.
Results may differ from the reference program's by a relative error of at most 0.0003.
Values may be sent and summed in bfloat16 or wider, within the bound.
No kernel may reach another device: no remote copies, remote signals or barrier semaphores. Data moves between devices by JAX's collectives and lax.ppermute only.
A program may use at most 64 MiB of HBM per device.

```python
import math
import jax
import jax.numpy as jnp
from jax import lax

DET = 2560
RY = 128
PIX = 1024
VB = 2
FRAMES = 2
SWEEPS = 3
TV_STEPS = 2
NZ = 1024
NV = 16
N_VIEW = 8


def draw_warm_volume(key, part):
    zpos = jnp.arange(NZ, dtype=jnp.float32) / max(NZ - 1, 1)
    amplitude = 0.15 * 3.0 ** zpos
    first_key = jax.random.fold_in(key, 0)
    noise = jax.random.uniform(first_key, (NZ, PIX), jnp.float32, minval=-1.0, maxval=1.0)
    return (1.0 + amplitude[:, None] * noise).astype(jnp.float32)


def shard_levels(rng, extent, cuts, smallest, largest):
    loudness = 1.0
    for dim, shards_of in cuts:
        steps = jax.random.uniform(jax.random.fold_in(jax.random.fold_in(rng, 6), dim), (shards_of,), jnp.float32, smallest / len(cuts), largest / len(cuts))
        loudness = loudness * jnp.repeat(jnp.exp(steps), extent[dim] // shards_of).reshape((-1,) + (1,) * (len(extent) - 1 - dim))
    return loudness


def setup_inputs(seed: int = 0) -> dict:
    streams_of = jax.random.split(jax.random.key(seed), 5)
    return {
        "sinogram": jnp.clip(102.0 + 256.0 * jax.random.uniform(streams_of[0], (FRAMES, NV, NZ, DET), jnp.float32) ** shard_levels(streams_of[0], (FRAMES, NV, NZ, DET), ((1, 8), (2, 16)), -0.2, 0.2), 102.0, 358.0).astype(jnp.bfloat16),
        "projector": jnp.clip(jnp.exp(math.log(1.0) - 4.61031033 * jax.random.uniform(streams_of[1], (NV, PIX, DET), jnp.float32) ** shard_levels(streams_of[1], (NV, PIX, DET), ((0, 8),), -0.2, 0.2)), 0.0099487305, 1.0).astype(jnp.bfloat16),
        "warm_volume": draw_warm_volume(jax.random.fold_in(streams_of[4], 71), 0),
        "view_order": jax.random.permutation(streams_of[3], VB).astype(jnp.int32),
    }


RELAXATION = 0.9
STEP_SCALE = 0.3
STEP_DECAY = 0.7
SMOOTHING = 0.01
NORM_GUARD = 1e-06

def tv_gradient(volume, first_z, depth_total):
    row_count = volume.shape[0]
    pixels = volume.shape[1]
    zero_row = jnp.zeros((1, pixels), jnp.float32)
    zero_band = jnp.zeros((row_count, RY), jnp.float32)
    zero_col = jnp.zeros((row_count, 1), jnp.float32)
    zindex = first_z + jnp.arange(row_count, dtype=jnp.int32)
    inside = ((zindex >= 0) & (zindex < depth_total - 1)).astype(jnp.float32)
    diff_z = jnp.concatenate([volume[1:] - volume[:-1], zero_row], axis=0) * inside[:, None]
    diff_i = jnp.concatenate([volume[:, RY:] - volume[:, :-RY], zero_band], axis=1)
    column = jnp.arange(pixels, dtype=jnp.int32) % RY
    diff_j = jnp.concatenate([volume[:, 1:] - volume[:, :-1], zero_col], axis=1)
    diff_j = diff_j * (column < RY - 1).astype(jnp.float32)[None, :]
    magnitude = jnp.sqrt(diff_z * diff_z + diff_i * diff_i + diff_j * diff_j + SMOOTHING)
    flux_z = diff_z / magnitude
    flux_i = diff_i / magnitude
    flux_j = diff_j / magnitude
    gradient = jnp.concatenate([zero_row, flux_z[:-1]], axis=0) - flux_z
    gradient = gradient + (jnp.concatenate([zero_band, flux_i[:, :-RY]], axis=1) - flux_i)
    gradient = gradient + (jnp.concatenate([zero_col, flux_j[:, :-1]], axis=1) - flux_j)
    return gradient

def superize(volume, first_step):
    for step_no in range(TV_STEPS):
        gradient = tv_gradient(volume, 0, NZ)
        spread = jnp.sqrt(jnp.sum(gradient * gradient) / (NZ * PIX) + NORM_GUARD)
        volume = volume - STEP_SCALE * STEP_DECAY ** (first_step + step_no) * gradient / spread
    return volume

def reference(sinogram, projector, warm_volume, view_order):
    tile_stack = projector.reshape(N_VIEW, VB, PIX, DET)
    ray_sums = lax.optimization_barrier(jnp.sum(tile_stack, axis=2, dtype=jnp.float32))
    coverage = lax.optimization_barrier(jnp.sum(tile_stack, axis=(0, 3), dtype=jnp.float32))
    frame_data = sinogram.reshape(FRAMES, N_VIEW, VB, NZ, DET)
    volume = warm_volume
    finished = []
    for frame_no in range(FRAMES):
        for sweep_no in range(SWEEPS):
            volume = superize(volume, sweep_no * TV_STEPS)
            for subset in range(VB):
                slot_index = view_order[subset]
                tiles = jnp.take(tile_stack, slot_index, axis=1)
                totals = jnp.take(ray_sums, slot_index, axis=1)
                observed = jnp.take(frame_data[frame_no], slot_index, axis=1)
                rounded = volume.astype(jnp.bfloat16)

                def backproject(items):
                    ray_tile, observed_rows, ray_total = items
                    forward = jnp.dot(rounded, ray_tile, preferred_element_type=jnp.float32)
                    mismatch = ((observed_rows.astype(jnp.float32) - forward) / ray_total[None, :]).astype(jnp.bfloat16)
                    return lax.dot_general(mismatch, ray_tile, (((1,), (1,)), ((), ())), preferred_element_type=jnp.float32)
                partial_back = lax.map(backproject, (tiles, observed, totals))
                summed = lax.optimization_barrier(jnp.sum(partial_back, axis=0))
                weight = jnp.take(coverage, slot_index, axis=0)
                volume = jnp.maximum(volume + RELAXATION * summed / weight[None, :], 0.0)
        finished.append(volume)
    return jnp.stack(finished, axis=0)
```

```python
import functools

import jax
import jax.numpy as jnp
from jax import lax
from jax.experimental import pallas as pl
from jax.experimental.pallas import tpu as pltpu
from jax.sharding import PartitionSpec as P

RY = 128
FRAMES = 2
SWEEPS = 3
TV_STEPS = 2
VIEW = 8
HALO = 16
CHUNK = 256

RELAXATION = 0.9
STEP_SCALE = 0.3
STEP_DECAY = 0.7
SMOOTHING = 0.01
NORM_GUARD = 1e-06

F32 = jnp.float32
BF16 = jnp.bfloat16
VMEM = pl.BlockSpec(memory_space=pltpu.VMEM)
SMEM = pl.BlockSpec(memory_space=pltpu.SMEM)


def params(**kw):
    return pltpu.CompilerParams(vmem_limit_bytes=56 * 1024 * 1024, **kw)


def gram_kernel(order_ref, slab_ref, a_ref, s0_ref, s1_ref, out_ref, acc):
    n = pl.program_id(0)
    d = pl.program_id(1)
    rows = s0_ref.shape[0]
    part = rows // VIEW
    tile = a_ref[...]
    ray = jnp.sum(tile.astype(F32), axis=0, keepdims=True)
    inverse = 1.0 / ray
    lhs = []
    low = []
    for ref in (s0_ref, s1_ref):
        scaled = ref[...].astype(F32) * inverse
        high = scaled.astype(BF16)
        lhs.append(high)
        low.append((scaled - high.astype(F32)).astype(BF16))
    mine = a_ref[pl.ds(pl.multiple_of(slab_ref[0] * rows, rows), rows), :]
    lhs.append((mine.astype(F32) * inverse).astype(BF16))
    lhs.append(jnp.ones((16, CHUNK), BF16))
    stack = jnp.concatenate(lhs + low, axis=0)
    product = lax.dot_general(stack, tile, (((1,), (1,)), ((), ())), preferred_element_type=F32)
    top = 3 * rows + 16

    @pl.when(d == 0)
    def _():
        acc[...] = product

    @pl.when(d > 0)
    def _():
        acc[...] += product

    @pl.when(d == pl.num_programs(1) - 1)
    def _():
        b0 = acc[0:rows] + acc[top : top + rows]
        b1 = acc[rows : 2 * rows] + acc[top + rows : top + 2 * rows]
        for v in range(VIEW):
            where = pl.ds(v * part, part)
            out_ref[v, pl.ds(pl.multiple_of(n * part, part), part), :] = b0[v * part : (v + 1) * part]
            out_ref[v, pl.ds(pl.multiple_of((2 + n) * part, part), part), :] = b1[
                v * part : (v + 1) * part
            ]

        wide = 2 * part
        for quarter in range(VIEW // 2):
            for half in range(2):
                @pl.when(n == half)
                def _():
                    out_ref[2 * quarter + half, 4 * part : 4 * part + wide, :] = acc[
                        2 * rows + quarter * wide : 2 * rows + (quarter + 1) * wide
                    ]
        for half in range(2):
            @pl.when(n == half)
            def _():
                row = acc[3 * rows : 3 * rows + 1]
                for v in range(VIEW):
                    out_ref[v, 6 * part + half : 6 * part + half + 1, :] = row


def gram_products(order, slab, projector, measured):
    _, pixels, det = projector.shape
    rows = measured.shape[2]
    part = rows // VIEW
    total = 5 * rows + 16
    out_rows = 7 * part
    return pl.pallas_call(
        gram_kernel,
        out_shape=jax.ShapeDtypeStruct((VIEW, out_rows, pixels), F32),
        grid_spec=pltpu.PrefetchScalarGridSpec(
            num_scalar_prefetch=2,
            grid=(2, det // CHUNK),
            in_specs=[
                pl.BlockSpec((None, pixels, CHUNK), lambda n, d, o, s: (o[n], 0, d)),
                pl.BlockSpec((None, None, rows, CHUNK), lambda n, d, o, s: (0, o[n], 0, d)),
                pl.BlockSpec((None, None, rows, CHUNK), lambda n, d, o, s: (1, o[n], 0, d)),
            ],
            out_specs=pl.BlockSpec((VIEW, out_rows, pixels), lambda n, d, o, s: (0, 0, 0)),
            scratch_shapes=[pltpu.VMEM((total, pixels), F32)],
        ),
        compiler_params=params(),
        name="gram_products",
    )(order, slab, projector, measured, measured)


def reduce_kernel(core_ref, got_ref, b_ref, g_ref, cov_ref):
    part = 8
    total = got_ref[0]
    for v in range(1, VIEW):
        total = total + got_ref[v]
    cov = total[6 * part : 6 * part + 2]
    scale = RELAXATION / cov
    b_ref[0] = total[0:part] * scale[0:1]
    b_ref[1] = total[part : 2 * part] * scale[1:2]
    b_ref[2] = total[2 * part : 3 * part] * scale[0:1]
    b_ref[3] = total[3 * part : 4 * part] * scale[1:2]
    gram = total[4 * part : 6 * part]
    mine = jnp.where(core_ref[0] == 0, cov[0:1], cov[1:2])
    own = jnp.sum(gram, axis=1, keepdims=True)
    weight = jnp.sum(mine, axis=1, keepdims=True)
    g_ref[...] = (gram - own * (mine / weight)).astype(BF16)
    cov_ref[...] = total[6 * part : 7 * part]


def reduce_views(core, got):
    pixels = got.shape[-1]
    return pl.pallas_call(
        reduce_kernel,
        out_shape=(
            jax.ShapeDtypeStruct((4, 8, pixels), F32),
            jax.ShapeDtypeStruct((16, pixels), BF16),
            jax.ShapeDtypeStruct((8, pixels), F32),
        ),
        in_specs=[SMEM, VMEM],
        out_specs=(VMEM, VMEM, VMEM),
        compiler_params=params(),
        name="reduce_views",
    )(core, got)


def tv_into(x_ref, g_ref, ss_ref, first, depth):
    height, pixels = x_ref.shape
    blocks = pixels // RY
    lane = lax.broadcasted_iota(jnp.int32, (height, RY), 1)
    zindex = first + lax.broadcasted_iota(jnp.int32, (height, RY), 0)
    inside = ((zindex >= 0) & (zindex < depth - 1)).astype(F32)
    column = (lane < RY - 1).astype(F32)
    before = None
    total = None
    here = x_ref[:, 0:RY]
    for i in range(blocks):
        dz = (pltpu.roll(here, height - 1, 0) - here) * inside
        dc = (pltpu.roll(here, RY - 1, 1) - here) * column
        square = dz * dz + dc * dc + SMOOTHING
        if i < blocks - 1:
            following = x_ref[:, (i + 1) * RY : (i + 2) * RY]
            di = following - here
            square = square + di * di
        r = lax.rsqrt(square)
        r = r * (1.5 - 0.5 * square * r * r)
        fz = dz * r
        fc = dc * r
        g = (pltpu.roll(fz, 1, 0) - fz) + (pltpu.roll(fc, 1, 1) - fc)
        if i < blocks - 1:
            fi = di * r
            g = g - fi
        if before is not None:
            g = g + before
        g_ref[:, i * RY : (i + 1) * RY] = g
        inner = g[HALO : height - HALO]
        piece = inner * inner
        total = piece if total is None else total + piece
        if i < blocks - 1:
            before = fi
            here = following
    folded = total[0:8]
    for k in range(1, total.shape[0] // 8):
        folded = folded + total[8 * k : 8 * k + 8]
    for k in range(ss_ref.shape[0]):
        ss_ref[k] = folded


def descend(x, g, sums, step, cells):
    total = jnp.sum(jnp.sum(sums, axis=0), axis=(0, 1), keepdims=True)
    spread = jnp.sqrt(total / cells + NORM_GUARD)
    return x - (STEP_SCALE * STEP_DECAY**step) * (g / spread)


def first_kernel(meta_ref, x_ref, g_ref, ss_ref, *, depth):
    tv_into(x_ref, g_ref, ss_ref, meta_ref[0], depth)


def second_kernel(meta_ref, x_ref, g_ref, sums_ref, x_out, g_out, ss_out, *, depth, step, cells):
    x_out[...] = descend(x_ref[...], g_ref[...], sums_ref[...], step, cells)
    tv_into(x_out, g_out, ss_out, meta_ref[0], depth)


def subset_kernel(
    meta_ref, x_ref, g_ref, sums_ref, gram_ref, b_ref, cov_ref, *outs, depth, step, cells, frame, last, final
):
    x = descend(x_ref[...], g_ref[...], sums_ref[...], step, cells)
    for n in range(2):
        rounded = x.astype(BF16)
        product = jnp.dot(rounded, gram_ref[n], preferred_element_type=F32)
        cov = cov_ref[n : n + 1, :]
        weight = jnp.sum(cov, axis=1, keepdims=True)
        along = jnp.sum(rounded.astype(F32) * cov, axis=1, keepdims=True)
        change = b_ref[2 * frame + n] - product * (RELAXATION / cov) - along * (RELAXATION / weight)
        x = jnp.maximum(x + change, 0.0)
    outs = list(outs)
    if last:
        volume_out = outs.pop(0)
        volume_out[...] = x[HALO : x.shape[0] - HALO]
    if not final:
        x_out, g_out, ss_out = outs
        x_out[...] = x
        tv_into(x_out, g_out, ss_out, meta_ref[0], depth)


def body(sinogram, projector, warm_volume, view_order):
    slices, pixels = warm_volume.shape
    slab_axes = ("tm", "gz")
    slabs = lax.axis_size("tm") * lax.axis_size("gz")
    slab = (lax.axis_index("tm") * lax.axis_size("gz") + lax.axis_index("gz")).astype(jnp.int32)
    view = lax.axis_index("view").astype(jnp.int32)
    depth = slices * slabs
    cells = depth * pixels
    height = slices + 2 * HALO
    meta = (slab * slices - HALO).reshape(1)

    up = [(i, i + 1) for i in range(slabs - 1)]
    down = [(b, a) for a, b in up]

    def widen(array, dim):
        length = array.shape[dim]
        low = lax.ppermute(lax.slice_in_dim(array, length - HALO, length, axis=dim), slab_axes, up)
        high = lax.ppermute(lax.slice_in_dim(array, 0, HALO, axis=dim), slab_axes, down)
        return jnp.concatenate([low, array, high], axis=dim)

    partial = gram_products(view_order, slab.reshape(1), projector, sinogram)
    got = lax.all_to_all(partial, "view", 0, 0, tiled=True)
    b_part, g_part, cov = reduce_views((view % 2).reshape(1), got)

    b_all = lax.all_to_all(
        jnp.broadcast_to(b_part[None], (VIEW, *b_part.shape)), "view", 0, 0, tiled=False
    )
    b_all = b_all.transpose(1, 0, 2, 3).reshape(4, slices, pixels)
    b_wide = widen(b_all, 1)

    lines = [g_part]
    for hop in (2, 4, 6):
        lines.append(lax.ppermute(g_part, "view", [(i, (i + hop) % VIEW) for i in range(VIEW)]))
    z = view // 2
    stack = jnp.stack(lines)
    stack = jnp.take(stack, (z - jnp.arange(4)) % 4, axis=0)
    strip = stack.reshape(slices, pixels)
    whole = lax.all_to_all(
        jnp.broadcast_to(strip[None], (slabs, *strip.shape)), slab_axes, 0, 0, tiled=True
    )
    mine = whole.reshape(depth, pixels)
    other = lax.ppermute(mine, "view", [(i, i ^ 1) for i in range(VIEW)])
    core = view % 2
    gram = jnp.stack([jnp.where(core == 0, mine, other), jnp.where(core == 0, other, mine)])

    shape = jax.ShapeDtypeStruct((height, pixels), F32)
    sums_shape = jax.ShapeDtypeStruct((slabs, 8, RY), F32)

    def everyone(sums):
        return lax.all_to_all(sums, slab_axes, 0, 0, tiled=True)

    x = widen(warm_volume, 0)
    g, sums = pl.pallas_call(
        functools.partial(first_kernel, depth=depth),
        out_shape=(shape, sums_shape),
        in_specs=[SMEM, VMEM],
        out_specs=(VMEM, VMEM),
        compiler_params=params(),
        name="first",
    )(meta, x)
    finished = []
    for frame in range(FRAMES):
        for sweep in range(SWEEPS):
            step = sweep * TV_STEPS
            x, g, sums = pl.pallas_call(
                functools.partial(second_kernel, depth=depth, step=step, cells=cells),
                out_shape=(shape, shape, sums_shape),
                in_specs=[SMEM, VMEM, VMEM, VMEM],
                out_specs=(VMEM, VMEM, VMEM),
                compiler_params=params(),
                name="second",
            )(meta, x, g, everyone(sums))
            last = sweep == SWEEPS - 1
            final = last and frame == FRAMES - 1
            out_shape = ()
            if last:
                out_shape += (jax.ShapeDtypeStruct((slices, pixels), F32),)
            if not final:
                out_shape += (shape, shape, sums_shape)
            outs = pl.pallas_call(
                functools.partial(
                    subset_kernel,
                    depth=depth,
                    step=step + 1,
                    cells=cells,
                    frame=frame,
                    last=last,
                    final=final,
                ),
                out_shape=out_shape,
                in_specs=[SMEM] + [VMEM] * 6,
                out_specs=tuple(VMEM for _ in out_shape),
                compiler_params=params(),
                name="subset",
            )(meta, x, g, everyone(sums), gram, b_wide, cov)
            outs = list(outs)
            if last:
                finished.append(outs.pop(0))
            if not final:
                x, g, sums = outs
    return jnp.stack(finished, axis=0)


def solution(mesh):
    return jax.shard_map(
        body,
        mesh=mesh,
        in_specs=(
            P(None, "view", ("tm", "gz"), None),
            P("view", None, None),
            P(("tm", "gz"), None),
            P(),
        ),
        out_specs=P(None, ("tm", "gz"), None),
        check_vma=False,
    )
```

```python
import functools

import jax
import jax.numpy as jnp
from jax import lax
from jax.experimental import pallas as pl
from jax.experimental.pallas import tpu as pltpu
from jax.sharding import PartitionSpec as P

RY = 128
FRAMES = 2
SWEEPS = 3
TV_STEPS = 2
HALO = 16
CHUNK = 512
QUARTERS = 4
AXES = ("tm", "gz", "view")

RELAXATION = 0.9
STEP_SCALE = 0.3
STEP_DECAY = 0.7
SMOOTHING = 0.01
NORM_GUARD = 1e-06

F32 = jnp.float32
BF16 = jnp.bfloat16
WHOLE = pl.BlockSpec(memory_space=pltpu.VMEM)
SCALARS = pl.BlockSpec(memory_space=pltpu.SMEM)


def params():
    return pltpu.CompilerParams(vmem_limit_bytes=40 * 1024 * 1024)


def near(array):
    return pltpu.with_memory_space_constraint(array, pltpu.VMEM)


def call(kernel, name, outs, ids, *arrays, scratch=()):
    return pl.pallas_call(
        kernel,
        out_shape=tuple(pltpu.VMEM(shape, dtype) for shape, dtype in outs),
        in_specs=[SCALARS] + [WHOLE] * len(arrays),
        out_specs=tuple(WHOLE for _ in outs),
        scratch_shapes=scratch,
        compiler_params=params(),
        name=name,
    )(ids, *[near(a) for a in arrays])


def keeps(d):
    return d[4] == d[1] // 2


def move(array, rule, source=None):
    pairs = []
    for tm in range(2):
        for y in range(4):
            for h in range(2):
                for z in range(4):
                    for c in range(2):
                        here = (tm, y, h, z, c)
                        if source is not None and not source(here):
                            continue
                        there = rule(*here)
                        if there is None:
                            continue
                        index = [((t * 4 + a) * 2 + b) * 8 + 2 * u + v for t, a, b, u, v in (here, there)]
                        pairs.append(tuple(index))
    return lax.ppermute(array, AXES, pairs)


def flip(dtm=0, dy=0, dh=0, dz=0, dc=0):
    return lambda tm, y, h, z, c: (tm ^ dtm, y ^ dy, h ^ dh, z ^ dz, c ^ dc)


def strip_step(step):
    def rule(tm, y, h, z, c):
        strip = 2 * tm + c + step
        return (strip // 2, y, h, z, strip % 2) if 0 <= strip < 4 else None

    return rule


def gram_kernel(order_ref, ids_ref, a_ref, s0_ref, s1_ref, b_ref, g_ref, acc):
    n = pl.program_id(0)
    d = pl.program_id(1)
    rows = s0_ref.shape[0]
    tile = a_ref[...]
    ray = jnp.sum(tile.astype(F32), axis=0, keepdims=True)
    inverse = 1.0 / ray
    lhs = []
    low = []
    for ref in (s0_ref, s1_ref):
        scaled = ref[...].astype(F32) * inverse
        high = scaled.astype(BF16)
        lhs.append(high)
        low.append((scaled - high.astype(F32)).astype(BF16))
    mine = a_ref[pl.ds(pl.multiple_of(ids_ref[1] * rows, rows), rows), :]
    lhs.append((mine.astype(F32) * inverse).astype(BF16))
    lhs.append(jnp.ones((16, CHUNK), BF16))
    stack = jnp.concatenate(lhs + low, axis=0)
    product = lax.dot_general(stack, tile, (((1,), (1,)), ((), ())), preferred_element_type=F32)
    top = 3 * rows + 16

    @pl.when(d == 0)
    def _():
        acc[...] = product

    @pl.when(d > 0)
    def _():
        acc[...] += product

    @pl.when(d == pl.num_programs(1) - 1)
    def _():
        part = rows // QUARTERS
        for quarter in range(QUARTERS):
            slot = jnp.bitwise_xor(ids_ref[2], quarter)
            for t in range(FRAMES):
                lo = t * rows + quarter * part
                value = acc[lo : lo + part] + acc[top + lo : top + lo + part]
                b_ref[slot, pl.ds(pl.multiple_of((2 * t + n) * part, part), part), :] = value
            lo = 2 * rows + quarter * part
            g_ref[slot, pl.ds(pl.multiple_of(n * part, part), part), :] = acc[lo : lo + part]
        for half in range(2):

            @pl.when(n == half)
            def _():
                cover = acc[3 * rows : 3 * rows + 8]
                for k in range(QUARTERS):
                    b_ref[k, 4 * part + half : 4 * part + 8, :] = cover[half:8]
                    g_ref[k, 2 * part + half : 2 * part + 8, :] = cover[half:8]


def gram_products(order, ids, projector, measured):
    _, pixels, det = projector.shape
    rows = measured.shape[2]
    part = rows // QUARTERS
    b_shape = (QUARTERS, 4 * part + 8, pixels)
    g_shape = (QUARTERS, 2 * part + 8, pixels)
    return pl.pallas_call(
        gram_kernel,
        out_shape=(jax.ShapeDtypeStruct(b_shape, F32), jax.ShapeDtypeStruct(g_shape, F32)),
        grid_spec=pltpu.PrefetchScalarGridSpec(
            num_scalar_prefetch=2,
            grid=(2, det // CHUNK),
            in_specs=[
                pl.BlockSpec((None, pixels, CHUNK), lambda n, d, o, s: (o[n], 0, d)),
                pl.BlockSpec((None, None, rows, CHUNK), lambda n, d, o, s: (0, o[n], 0, d)),
                pl.BlockSpec((None, None, rows, CHUNK), lambda n, d, o, s: (1, o[n], 0, d)),
            ],
            out_specs=(
                pl.BlockSpec(b_shape, lambda n, d, o, s: (0, 0, 0)),
                pl.BlockSpec(g_shape, lambda n, d, o, s: (0, 0, 0)),
            ),
            scratch_shapes=[pltpu.VMEM((5 * rows + 16, pixels), F32)],
        ),
        compiler_params=params(),
        name="gram_products",
    )(order, ids, projector, measured, measured)


def reduce_kernel(ids_ref, b0, b1, b2, b3, g0, g1, g2, g3, first_ref, second_ref, gram_ref, aux_ref):
    part = gram_ref.shape[1]
    b = (b0[...] + b1[...]) + (b2[...] + b3[...])
    g = (g0[...] + g1[...]) + (g2[...] + g3[...])
    keeper = ids_ref[4] == 1
    cov = jnp.where(keeper, b[4 * part : 4 * part + 8], g[2 * part : 2 * part + 8])
    scale = RELAXATION / cov
    for t, ref in enumerate((first_ref, second_ref)):
        for n in range(2):
            lo = (2 * t + n) * part
            ref[n] = b[lo : lo + part] * scale[n : n + 1]
    for n in range(2):
        rows = g[n * part : (n + 1) * part]
        share = cov[n : n + 1] / jnp.sum(cov[n : n + 1], axis=1, keepdims=True)
        own = jnp.sum(rows, axis=1, keepdims=True)
        gram_ref[n] = (rows - own * share).astype(BF16)
        aux_ref[n : n + 1] = RELAXATION * share
        aux_ref[2 + n : 3 + n] = scale[n : n + 1]


def place_gram_kernel(ids_ref, y0, y1, y2, y3, out_ref):
    z, y, h, tm = ids_ref[2], ids_ref[5], ids_ref[6], ids_ref[7]
    part = y0.shape[1]
    for dy, ref in enumerate((y0, y1, y2, y3)):
        for dx in range(4):
            slab = (
                jnp.bitwise_xor(tm, dx // 2) * 8
                + jnp.bitwise_xor(y, dy) * 2
                + jnp.bitwise_xor(h, dx % 2)
            )
            for k in range(QUARTERS):
                row = slab * (QUARTERS * part) + jnp.bitwise_xor(z, k) * part
                out_ref[pl.ds(pl.multiple_of(row, part), part), :] = ref[dx * QUARTERS + k]


def place_rows_kernel(ids_ref, z0, z1, z2, z3, out_ref):
    z = ids_ref[2]
    part = z0.shape[2]
    for k, ref in enumerate((z0, z1, z2, z3)):
        start = jnp.bitwise_xor(z, k) * part
        for slab in range(4):
            for n in range(2):
                row = slab * (QUARTERS * part) + start
                out_ref[n, pl.ds(pl.multiple_of(row, part), part), :] = ref[slab, n]


def tv_into(x_ref, g_ref, ss_ref, flux_ref, first, depth):
    height, pixels = x_ref.shape
    blocks = pixels // RY
    lane = lax.broadcasted_iota(jnp.int32, (height, RY), 1)
    zindex = first + lax.broadcasted_iota(jnp.int32, (height, RY), 0)
    inside = ((zindex >= 0) & (zindex < depth - 1)).astype(F32)
    column = (lane < RY - 1).astype(F32)
    flux_ref[...] = jnp.zeros_like(flux_ref)

    def block(i, folded):
        here_at = pl.ds(pl.multiple_of(i * RY, RY), RY)
        next_at = pl.ds(pl.multiple_of(jnp.minimum(i + 1, blocks - 1) * RY, RY), RY)
        here = x_ref[:, here_at]
        dz = (pltpu.roll(here, height - 1, 0) - here) * inside
        dc = (pltpu.roll(here, RY - 1, 1) - here) * column
        di = x_ref[:, next_at] - here
        square = dz * dz + dc * dc + di * di + SMOOTHING
        r = lax.rsqrt(square)
        r = r * (1.5 - 0.5 * square * r * r)
        fz = dz * r
        fc = dc * r
        fi = di * r
        g = (pltpu.roll(fz, 1, 0) - fz) + (flux_ref[...] - fi) + (pltpu.roll(fc, 1, 1) - fc)
        flux_ref[...] = fi
        g_ref[:, here_at] = g
        inner = g[HALO : height - HALO]
        piece = inner * inner
        for k in range(piece.shape[0] // 8):
            folded = folded + piece[8 * k : 8 * k + 8]
        return folded

    ss_ref[...] = lax.fori_loop(0, blocks, block, jnp.zeros((8, RY), F32))


def descend(x_ref, g_ref, sums, step, cells):
    folded = (sums[0][...] + sums[1][...]) + (sums[2][...] + sums[3][...])
    total = jnp.sum(folded, axis=(0, 1), keepdims=True)
    factor = (STEP_SCALE * STEP_DECAY**step) / jnp.sqrt(total / cells + NORM_GUARD)
    return x_ref[...] - factor * g_ref[...]


def first_kernel(ids_ref, x_ref, g_ref, ss_ref, flux, *, depth):
    tv_into(x_ref, g_ref, ss_ref, flux, ids_ref[0], depth)


def second_kernel(ids_ref, x_ref, g_ref, s0, s1, s2, s3, x_out, g_out, ss_out, flux, *, depth, step, cells):
    x_out[...] = descend(x_ref, g_ref, (s0, s1, s2, s3), step, cells)
    tv_into(x_out, g_out, ss_out, flux, ids_ref[0], depth)


def subset_kernel(
    ids_ref, x_ref, g_ref, s0, s1, s2, s3, mine_ref, other_ref, b_ref, aux_ref, *rest, depth, step, cells, final
):
    flux, product = rest[-2:]
    x_out = rest[0]
    height = x_ref.shape[0]
    x_out[...] = descend(x_ref, g_ref, (s0, s1, s2, s3), step, cells)
    core = ids_ref[3]

    def subset(n, carry):
        rounded = x_out[...].astype(BF16)

        @pl.when(n == core)
        def _():
            product[...] = jnp.dot(rounded, mine_ref[...], preferred_element_type=F32)

        @pl.when(n != core)
        def _():
            product[...] = jnp.dot(rounded, other_ref[...], preferred_element_type=F32)

        along = jnp.sum(rounded.astype(F32) * aux_ref[pl.ds(n, 1), :], axis=1, keepdims=True)
        change = b_ref[n] - product[...] * aux_ref[pl.ds(2 + n, 1), :] - along
        x_out[...] = jnp.maximum(x_out[...] + change, 0.0)
        return carry

    lax.fori_loop(0, 2, subset, 0)
    if not final:
        g_out, ss_out = rest[1:3]
        tv_into(x_out, g_out, ss_out, flux, ids_ref[0], depth)


def body(sinogram, projector, warm_volume, view_order):
    slices, pixels = warm_volume.shape
    part = slices // QUARTERS
    tm = lax.axis_index("tm").astype(jnp.int32)
    gz = lax.axis_index("gz").astype(jnp.int32)
    view = lax.axis_index("view").astype(jnp.int32)
    y, h = gz // 2, gz % 2
    z, c = view // 2, view % 2
    slab = tm * 8 + gz
    keeper = c == y // 2
    depth = slices * 16
    cells = depth * pixels
    inner = 4 * slices
    height = inner + 2 * HALO
    first = (2 * tm + c) * inner - HALO
    ids = jnp.stack([first, slab, z, c, keeper.astype(jnp.int32), y, h, tm])

    def slabs_of_strip(unit):
        across = move(unit, flip(dh=1), keeps)
        pair = jnp.where(h == 0, jnp.stack([unit, across]), jnp.stack([across, unit]))
        one = move(pair, flip(dy=1), keeps)
        two = move(pair, flip(dy=2), keeps)
        three = move(pair, flip(dy=3), keeps)
        same = jnp.where(keeper, pair, two)
        flipped = jnp.where(keeper, one, three)
        return jnp.where(
            y % 2 == 0, jnp.concatenate([same, flipped]), jnp.concatenate([flipped, same])
        )

    def widen(array, dim):
        length = array.shape[dim]
        low = move(lax.slice_in_dim(array, length - HALO, length, axis=dim), strip_step(1))
        high = move(lax.slice_in_dim(array, 0, HALO, axis=dim), strip_step(-1))
        return jnp.concatenate([low, array, high], axis=dim)

    partial_b, partial_g = gram_products(view_order, ids, projector, sinogram)
    got_b = move(partial_b, flip(dc=1), lambda d: not keeps(d))
    got_g = move(partial_g, flip(dc=1), keeps)
    b_terms = [partial_b[0] + got_b[0]]
    g_terms = [partial_g[0] + got_g[0]]
    for k in range(1, QUARTERS):
        b_terms.append(move(partial_b[k] + got_b[k], flip(dz=k), keeps))
        g_terms.append(move(partial_g[k] + got_g[k], flip(dz=k), lambda d: not keeps(d)))
    unit = ((2, part, pixels), F32)
    b_first, b_second, g_unit, aux = call(
        reduce_kernel,
        "reduce_views",
        [unit, unit, ((2, part, pixels), BF16), ((8, pixels), F32)],
        ids,
        *b_terms,
        *g_terms,
    )

    swapped = move(jnp.where(c == 0, g_unit[1], g_unit[0]), flip(dc=1), lambda d: not keeps(d))
    piece = jnp.where(keeper, swapped, jnp.where(c == 0, g_unit[0], g_unit[1]))
    line = jnp.stack([piece] + [move(piece, flip(dz=k)) for k in range(1, 4)])
    plane = jnp.concatenate(
        [line, move(line, flip(dh=1)), move(line, flip(dtm=1)), move(line, flip(dtm=1, dh=1))]
    )
    spread = [plane] + [move(plane, flip(dy=k)) for k in range(1, 4)]
    (mine,) = call(
        place_gram_kernel, "place_gram", [((slices * 16, pixels), BF16)], ids, *spread
    )
    other = move(mine, flip(dc=1))

    def b_rows(unit_b):
        strip = slabs_of_strip(unit_b)
        quarters = [strip] + [move(strip, flip(dz=k)) for k in range(1, 4)]
        (rows,) = call(place_rows_kernel, "place_rows", [((2, inner, pixels), F32)], ids, *quarters)
        return widen(rows, 1)

    b_wide = [b_rows(b_first), b_rows(b_second)]

    big = ((height, pixels), F32)
    small = ((8, RY), F32)
    flux = pltpu.VMEM((height, RY), F32)

    def everyone(sums):
        return [
            sums,
            move(sums, flip(dc=1)),
            move(sums, flip(dtm=1)),
            move(sums, flip(dtm=1, dc=1)),
        ]

    x = widen(slabs_of_strip(warm_volume).reshape(inner, pixels), 0)
    g, sums = call(
        functools.partial(first_kernel, depth=depth), "first", [big, small], ids, x, scratch=[flux]
    )
    finished = []
    for frame in range(FRAMES):
        for sweep in range(SWEEPS):
            step = sweep * TV_STEPS
            x, g, sums = call(
                functools.partial(second_kernel, depth=depth, step=step, cells=cells),
                "second",
                [big, big, small],
                ids,
                x,
                g,
                *everyone(sums),
                scratch=[flux],
            )
            final = sweep == SWEEPS - 1 and frame == FRAMES - 1
            outs = call(
                functools.partial(subset_kernel, depth=depth, step=step + 1, cells=cells, final=final),
                "subset",
                [big] if final else [big, big, small],
                ids,
                x,
                g,
                *everyone(sums),
                mine,
                other,
                b_wide[frame],
                aux,
                scratch=[flux, pltpu.VMEM((height, pixels), F32)],
            )
            if final:
                x = outs[0]
            else:
                x, g, sums = outs
        start = HALO + (gz % 4) * slices
        local = lax.dynamic_slice_in_dim(x, start, slices, axis=0)
        theirs = lax.dynamic_slice_in_dim(x, HALO + (gz % 4) * slices, slices, axis=0)
        passed = move(theirs, flip(dc=1), keeps)
        finished.append(jnp.where(keeper, local, passed))
    return jnp.stack(finished, axis=0)


def solution(mesh):
    return jax.shard_map(
        body,
        mesh=mesh,
        in_specs=(
            P(None, "view", ("tm", "gz"), None),
            P("view", None, None),
            P(("tm", "gz"), None),
            P(),
        ),
        out_specs=P(None, ("tm", "gz"), None),
        check_vma=False,
    )
```

```python
import functools

import jax
import jax.numpy as jnp
from jax import lax
from jax.experimental import pallas as pl
from jax.experimental.pallas import tpu as pltpu
from jax.sharding import PartitionSpec as P

RY = 128
FRAMES = 2
SWEEPS = 3
TV_STEPS = 2
HALO = 16
CHUNK = 512
QUARTERS = 4
AXES = ("tm", "gz", "view")

RELAXATION = 0.9
STEP_SCALE = 0.3
STEP_DECAY = 0.7
SMOOTHING = 0.01
NORM_GUARD = 1e-06

F32 = jnp.float32
BF16 = jnp.bfloat16
WHOLE = pl.BlockSpec(memory_space=pltpu.VMEM)
SCALARS = pl.BlockSpec(memory_space=pltpu.SMEM)


def params(mib):
    return pltpu.CompilerParams(vmem_limit_bytes=mib * 1024 * 1024)


def near(array):
    return pltpu.with_memory_space_constraint(array, pltpu.VMEM)


def call(kernel, name, outs, ids, *arrays, scratch=()):
    return pl.pallas_call(
        kernel,
        out_shape=tuple(pltpu.VMEM(shape, dtype) for shape, dtype in outs),
        in_specs=[SCALARS] + [WHOLE] * len(arrays),
        out_specs=tuple(WHOLE for _ in outs),
        scratch_shapes=scratch,
        compiler_params=params(12),
        name=name,
    )(ids, *[near(a) for a in arrays])


def keeps(d):
    return d[4] == d[1] // 2


def move(array, rule, source=None):
    pairs = []
    for tm in range(2):
        for y in range(4):
            for h in range(2):
                for z in range(4):
                    for c in range(2):
                        here = (tm, y, h, z, c)
                        if source is not None and not source(here):
                            continue
                        there = rule(*here)
                        if there is None:
                            continue
                        index = [((t * 4 + a) * 2 + b) * 8 + 2 * u + v for t, a, b, u, v in (here, there)]
                        pairs.append(tuple(index))
    return lax.ppermute(array, AXES, pairs)


def after(array, *others):
    return lax.optimization_barrier((array, *others))[0]


def flip(dtm=0, dy=0, dh=0, dz=0, dc=0):
    return lambda tm, y, h, z, c: (tm ^ dtm, y ^ dy, h ^ dh, z ^ dz, c ^ dc)


def strip_step(step):
    def rule(tm, y, h, z, c):
        strip = 2 * tm + c + step
        return (strip // 2, y, h, z, strip % 2) if 0 <= strip < 4 else None

    return rule


def gram_kernel(order_ref, ids_ref, a_ref, s0_ref, s1_ref, own_ref, send_ref, acc):
    n = pl.program_id(0)
    d = pl.program_id(1)
    rows = s0_ref.shape[0]
    tile = a_ref[...]
    ray = jnp.sum(tile.astype(F32), axis=0, keepdims=True)
    inverse = 1.0 / ray
    lhs = []
    low = []
    for ref in (s0_ref, s1_ref):
        scaled = ref[...].astype(F32) * inverse
        high = scaled.astype(BF16)
        lhs.append(high)
        low.append((scaled - high.astype(F32)).astype(BF16))
    mine = a_ref[pl.ds(pl.multiple_of(ids_ref[1] * rows, rows), rows), :]
    lhs.append((mine.astype(F32) * inverse).astype(BF16))
    lhs.append(jnp.ones((16, CHUNK), BF16))
    stack = jnp.concatenate(lhs + low, axis=0)
    product = lax.dot_general(stack, tile, (((1,), (1,)), ((), ())), preferred_element_type=F32)
    top = 3 * rows + 16

    @pl.when(d == 0)
    def _():
        acc[...] = product

    @pl.when(d > 0)
    def _():
        acc[...] += product

    @pl.when(d == pl.num_programs(1) - 1)
    def _():
        part = rows // QUARTERS
        at = pl.ds(pl.multiple_of(n * part, part), part)
        for t in range(FRAMES):
            for ref, who in ((own_ref, 1 - t), (send_ref, t)):

                @pl.when(ids_ref[4] == who)
                def _():
                    for quarter in range(QUARTERS):
                        lo = t * rows + quarter * part
                        ref[jnp.bitwise_xor(ids_ref[2], quarter), at, :] = (
                            acc[lo : lo + part] + acc[top + lo : top + lo + part]
                        )

        for ref, mine_too in ((own_ref, True), (send_ref, False)):

            @pl.when((ids_ref[3] == n) == mine_too)
            def _():
                for quarter in range(QUARTERS):
                    lo = 2 * rows + quarter * part
                    ref[jnp.bitwise_xor(ids_ref[2], quarter), 2 * part : 3 * part, :] = acc[lo : lo + part]

            for half in range(2):

                @pl.when(n == half)
                def _():
                    cover = acc[3 * rows : 3 * rows + 8]
                    for k in range(QUARTERS):
                        ref[k, 3 * part + half : 3 * part + 8, :] = cover[half:8]


def gram_products(order, ids, projector, measured):
    _, pixels, det = projector.shape
    rows = measured.shape[2]
    part = rows // QUARTERS
    shape = (QUARTERS, 3 * part + 8, pixels)
    out = pl.BlockSpec(shape, lambda n, d, o, s: (0, 0, 0))
    projector = pltpu.with_memory_space_constraint(projector, pltpu.HBM)
    measured = pltpu.with_memory_space_constraint(measured, pltpu.HBM)
    return pl.pallas_call(
        gram_kernel,
        out_shape=(jax.ShapeDtypeStruct(shape, F32),) * 2,
        grid_spec=pltpu.PrefetchScalarGridSpec(
            num_scalar_prefetch=2,
            grid=(2, det // CHUNK),
            in_specs=[
                pl.BlockSpec((None, pixels, CHUNK), lambda n, d, o, s: (o[n], 0, d)),
                pl.BlockSpec((None, None, rows, CHUNK), lambda n, d, o, s: (0, o[n], 0, d)),
                pl.BlockSpec((None, None, rows, CHUNK), lambda n, d, o, s: (1, o[n], 0, d)),
            ],
            out_specs=(out, out),
            scratch_shapes=[pltpu.VMEM((5 * rows + 16, pixels), F32)],
        ),
        compiler_params=params(24),
        name="gram_products",
    )(order, ids, projector, measured, measured)


def reduce_kernel(ids_ref, a0, a1, a2, a3, b_ref, gram_ref, aux_ref):
    part = gram_ref.shape[0]
    total = (a0[...] + a1[...]) + (a2[...] + a3[...])
    cov = total[3 * part : 3 * part + 8]
    scale = RELAXATION / cov
    share = cov / jnp.sum(cov, axis=1, keepdims=True)
    for n in range(2):
        b_ref[n] = total[n * part : (n + 1) * part] * scale[n : n + 1]
        aux_ref[n : n + 1] = RELAXATION * share[n : n + 1]
        aux_ref[2 + n : 3 + n] = scale[n : n + 1]
    rows = total[2 * part : 3 * part]
    own = jnp.sum(rows, axis=1, keepdims=True)
    mine = jnp.where(ids_ref[3] == 0, share[0:1], share[1:2])
    gram_ref[...] = (rows - own * mine).astype(BF16)


def place_gram_kernel(ids_ref, y0, y1, y2, y3, out_ref):
    z, y, h, tm = ids_ref[2], ids_ref[5], ids_ref[6], ids_ref[7]
    part = y0.shape[1]
    for dy, ref in enumerate((y0, y1, y2, y3)):
        for dx in range(4):
            slab = (
                jnp.bitwise_xor(tm, dx // 2) * 8
                + jnp.bitwise_xor(y, dy) * 2
                + jnp.bitwise_xor(h, dx % 2)
            )
            for k in range(QUARTERS):
                row = slab * (QUARTERS * part) + jnp.bitwise_xor(z, k) * part
                out_ref[pl.ds(pl.multiple_of(row, part), part), :] = ref[dx * QUARTERS + k]


def place_rows_kernel(ids_ref, z0, z1, z2, z3, out_ref):
    z = ids_ref[2]
    part = z0.shape[2]
    for k, ref in enumerate((z0, z1, z2, z3)):
        start = jnp.bitwise_xor(z, k) * part
        for slab in range(4):
            for n in range(2):
                row = slab * (QUARTERS * part) + start
                out_ref[n, pl.ds(pl.multiple_of(row, part), part), :] = ref[slab, n]


def tv_into(x_ref, g_ref, ss_ref, flux_ref, first, depth):
    height, pixels = x_ref.shape
    blocks = pixels // RY
    lane = lax.broadcasted_iota(jnp.int32, (height, RY), 1)
    zindex = first + lax.broadcasted_iota(jnp.int32, (height, RY), 0)
    inside = ((zindex >= 0) & (zindex < depth - 1)).astype(F32)
    column = (lane < RY - 1).astype(F32)
    flux_ref[...] = jnp.zeros_like(flux_ref)

    def block(i, folded):
        here_at = pl.ds(pl.multiple_of(i * RY, RY), RY)
        next_at = pl.ds(pl.multiple_of(jnp.minimum(i + 1, blocks - 1) * RY, RY), RY)
        here = x_ref[:, here_at]
        dz = (pltpu.roll(here, height - 1, 0) - here) * inside
        dc = (pltpu.roll(here, RY - 1, 1) - here) * column
        di = x_ref[:, next_at] - here
        square = dz * dz + dc * dc + di * di + SMOOTHING
        r = lax.rsqrt(square)
        r = r * (1.5 - 0.5 * square * r * r)
        fz = dz * r
        fc = dc * r
        fi = di * r
        g = (pltpu.roll(fz, 1, 0) - fz) + (flux_ref[...] - fi) + (pltpu.roll(fc, 1, 1) - fc)
        flux_ref[...] = fi
        g_ref[:, here_at] = g
        inner = g[HALO : height - HALO]
        piece = inner * inner
        for k in range(piece.shape[0] // 8):
            folded = folded + piece[8 * k : 8 * k + 8]
        return folded

    ss_ref[...] = lax.fori_loop(0, blocks, block, jnp.zeros((8, RY), F32))


def descend(x_ref, g_ref, sums, step, cells):
    folded = (sums[0][...] + sums[1][...]) + (sums[2][...] + sums[3][...])
    total = jnp.sum(folded, axis=(0, 1), keepdims=True)
    factor = (STEP_SCALE * STEP_DECAY**step) / jnp.sqrt(total / cells + NORM_GUARD)
    return x_ref[...] - factor * g_ref[...]


def first_kernel(ids_ref, x_ref, g_ref, ss_ref, flux, *, depth):
    tv_into(x_ref, g_ref, ss_ref, flux, ids_ref[0], depth)


def second_kernel(ids_ref, x_ref, g_ref, s0, s1, s2, s3, x_out, g_out, ss_out, flux, *, depth, step, cells):
    x_out[...] = descend(x_ref, g_ref, (s0, s1, s2, s3), step, cells)
    tv_into(x_out, g_out, ss_out, flux, ids_ref[0], depth)


def subset_kernel(
    ids_ref, x_ref, g_ref, s0, s1, s2, s3, mine_ref, other_ref, b_ref, aux_ref, *rest, depth, step, cells, final
):
    flux, product = rest[-2:]
    x_out = rest[0]
    height = x_ref.shape[0]
    x_out[...] = descend(x_ref, g_ref, (s0, s1, s2, s3), step, cells)
    core = ids_ref[3]

    def subset(n, carry):
        rounded = x_out[...].astype(BF16)

        @pl.when(n == core)
        def _():
            product[...] = jnp.dot(rounded, mine_ref[...], preferred_element_type=F32)

        @pl.when(n != core)
        def _():
            product[...] = jnp.dot(rounded, other_ref[...], preferred_element_type=F32)

        along = jnp.sum(rounded.astype(F32) * aux_ref[pl.ds(n, 1), :], axis=1, keepdims=True)
        change = b_ref[n] - product[...] * aux_ref[pl.ds(2 + n, 1), :] - along
        x_out[...] = jnp.maximum(x_out[...] + change, 0.0)
        return carry

    lax.fori_loop(0, 2, subset, 0)
    if not final:
        g_out, ss_out = rest[1:3]
        tv_into(x_out, g_out, ss_out, flux, ids_ref[0], depth)


def body(sinogram, projector, warm_volume, view_order):
    slices, pixels = warm_volume.shape
    part = slices // QUARTERS
    tm = lax.axis_index("tm").astype(jnp.int32)
    gz = lax.axis_index("gz").astype(jnp.int32)
    view = lax.axis_index("view").astype(jnp.int32)
    y, h = gz // 2, gz % 2
    z, c = view // 2, view % 2
    slab = tm * 8 + gz
    keeper = c == y // 2
    depth = slices * 16
    cells = depth * pixels
    inner = 4 * slices
    height = inner + 2 * HALO
    first = (2 * tm + c) * inner - HALO
    ids = jnp.stack([first, slab, z, c, keeper.astype(jnp.int32), y, h, tm])

    def slabs_of_strip(unit):
        across = move(unit, flip(dh=1), keeps)
        pair = jnp.where(h == 0, jnp.stack([unit, across]), jnp.stack([across, unit]))
        one = move(pair, flip(dy=1), keeps)
        two = move(pair, flip(dy=2), keeps)
        three = move(pair, flip(dy=3), keeps)
        same = jnp.where(keeper, pair, two)
        flipped = jnp.where(keeper, one, three)
        return jnp.where(
            y % 2 == 0, jnp.concatenate([same, flipped]), jnp.concatenate([flipped, same])
        )

    def widen(array, dim):
        length = array.shape[dim]
        low = move(lax.slice_in_dim(array, length - HALO, length, axis=dim), strip_step(1))
        high = move(lax.slice_in_dim(array, 0, HALO, axis=dim), strip_step(-1))
        return jnp.concatenate([low, array, high], axis=dim)

    own, send = gram_products(view_order, ids, projector, sinogram)
    both = own + move(send, flip(dc=1))
    terms = [both[0]] + [move(both[k], flip(dz=k)) for k in range(1, QUARTERS)]
    b_unit, piece, aux = call(
        reduce_kernel,
        "reduce_views",
        [((2, part, pixels), F32), ((part, pixels), BF16), ((8, pixels), F32)],
        ids,
        *terms,
    )

    line = jnp.stack([piece] + [move(piece, flip(dz=k)) for k in range(1, 4)])
    plane = jnp.concatenate(
        [line, move(line, flip(dh=1)), move(line, flip(dtm=1)), move(line, flip(dtm=1, dh=1))]
    )
    spread = [move(plane, flip(dy=k)) for k in range(1, 4)]

    def b_strip(unit_b):
        strip = slabs_of_strip(unit_b)
        return [strip] + [move(strip, flip(dz=k)) for k in range(1, 4)]

    def b_rows(quarters):
        (rows,) = call(place_rows_kernel, "place_rows", [((2, inner, pixels), F32)], ids, *quarters)
        return widen(rows, 1)

    quarters = b_strip(b_unit)

    big = ((height, pixels), F32)
    small = ((8, RY), F32)
    flux = pltpu.VMEM((height, RY), F32)

    def everyone(sums):
        return [
            sums,
            move(sums, flip(dc=1)),
            move(sums, flip(dtm=1)),
            move(sums, flip(dtm=1, dc=1)),
        ]

    x = widen(slabs_of_strip(after(warm_volume, both)).reshape(inner, pixels), 0)
    g, sums = call(
        functools.partial(first_kernel, depth=depth), "first", [big, small], ids, x, scratch=[flux]
    )
    b_wide = [None, None]
    finished = []
    for frame in range(FRAMES):
        for sweep in range(SWEEPS):
            step = sweep * TV_STEPS
            x, g, sums = call(
                functools.partial(second_kernel, depth=depth, step=step, cells=cells),
                "second",
                [big, big, small],
                ids,
                x,
                g,
                *everyone(sums),
                scratch=[flux],
            )
            if frame == 0 and sweep == 0:
                (mine,) = call(
                    place_gram_kernel,
                    "place_gram",
                    [((slices * 16, pixels), BF16)],
                    ids,
                    after(plane, sums),
                    *spread,
                )
                other = move(mine, flip(dc=1))
                b_wide[0] = b_rows(quarters)
            if frame == 0 and sweep == 1:
                later = move(after(b_unit, x), flip(dc=1), lambda d: not keeps(d))
                b_wide[1] = b_rows(b_strip(later))
            final = sweep == SWEEPS - 1 and frame == FRAMES - 1
            outs = call(
                functools.partial(subset_kernel, depth=depth, step=step + 1, cells=cells, final=final),
                "subset",
                [big] if final else [big, big, small],
                ids,
                x,
                g,
                *everyone(sums),
                mine,
                other,
                b_wide[frame],
                aux,
                scratch=[flux, pltpu.VMEM((height, pixels), F32)],
            )
            if final:
                x = outs[0]
            else:
                x, g, sums = outs
        start = HALO + (gz % 4) * slices
        local = lax.dynamic_slice_in_dim(x, start, slices, axis=0)
        passed = move(local, flip(dc=1), keeps)
        finished.append(jnp.where(keeper, local, passed))
    return jnp.stack(finished, axis=0)


def solution(mesh):
    return jax.shard_map(
        body,
        mesh=mesh,
        in_specs=(
            P(None, "view", ("tm", "gz"), None),
            P("view", None, None),
            P(("tm", "gz"), None),
            P(),
        ),
        out_specs=P(None, ("tm", "gz"), None),
        check_vma=False,
    )
```

```python
import functools

import jax
import jax.numpy as jnp
from jax import lax
from jax.experimental import pallas as pl
from jax.experimental.pallas import tpu as pltpu
from jax.sharding import PartitionSpec as P

RY = 128
FRAMES = 2
SWEEPS = 3
TV_STEPS = 2
HALO = 16
CHUNK = 512
QUARTERS = 4
AXES = ("tm", "gz", "view")

RELAXATION = 0.9
STEP_SCALE = 0.3
STEP_DECAY = 0.7
SMOOTHING = 0.01
NORM_GUARD = 1e-06

F32 = jnp.float32
BF16 = jnp.bfloat16
WHOLE = pl.BlockSpec(memory_space=pltpu.VMEM)
SCALARS = pl.BlockSpec(memory_space=pltpu.SMEM)


def params(mib):
    return pltpu.CompilerParams(vmem_limit_bytes=mib * 1024 * 1024)


def near(array):
    return pltpu.with_memory_space_constraint(array, pltpu.VMEM)


def call(kernel, outs, ids, *arrays, scratch=()):
    return pl.pallas_call(
        kernel,
        out_shape=tuple(pltpu.VMEM(shape, dtype) for shape, dtype in outs),
        in_specs=[SCALARS] + [WHOLE] * len(arrays),
        out_specs=tuple(WHOLE for _ in outs),
        scratch_shapes=scratch,
        compiler_params=params(12),
    )(ids, *[near(a) for a in arrays])


def keeps(d):
    return d[4] == d[1] // 2


def move(array, rule, source=None):
    pairs = []
    for tm in range(2):
        for y in range(4):
            for h in range(2):
                for z in range(4):
                    for c in range(2):
                        here = (tm, y, h, z, c)
                        if source is not None and not source(here):
                            continue
                        there = rule(*here)
                        if there is None:
                            continue
                        index = [((t * 4 + a) * 2 + b) * 8 + 2 * u + v for t, a, b, u, v in (here, there)]
                        pairs.append(tuple(index))
    return lax.ppermute(array, AXES, pairs)


def after(array, *others):
    return lax.optimization_barrier((array, *others))[0]


def flip(dtm=0, dy=0, dh=0, dz=0, dc=0):
    return lambda tm, y, h, z, c: (tm ^ dtm, y ^ dy, h ^ dh, z ^ dz, c ^ dc)


def strip_step(step):
    def rule(tm, y, h, z, c):
        strip = 2 * tm + c + step
        return (strip // 2, y, h, z, strip % 2) if 0 <= strip < 4 else None

    return rule


def gram_kernel(order_ref, ids_ref, a_ref, s0_ref, s1_ref, own_ref, send_ref, acc):
    n = pl.program_id(0)
    d = pl.program_id(1)
    rows = s0_ref.shape[0]
    tile = a_ref[...]
    ray = jnp.sum(tile.astype(F32), axis=0, keepdims=True)
    inverse = 1.0 / ray
    lhs = []
    low = []
    for ref in (s0_ref, s1_ref):
        scaled = ref[...].astype(F32) * inverse
        high = scaled.astype(BF16)
        lhs.append(high)
        low.append((scaled - high.astype(F32)).astype(BF16))
    mine = a_ref[pl.ds(pl.multiple_of(ids_ref[1] * rows, rows), rows), :]
    lhs.append((mine.astype(F32) * inverse).astype(BF16))
    lhs.append(jnp.ones((16, CHUNK), BF16))
    stack = jnp.concatenate(lhs + low, axis=0)
    product = lax.dot_general(stack, tile, (((1,), (1,)), ((), ())), preferred_element_type=F32)
    top = 3 * rows + 16

    @pl.when(d == 0)
    def _():
        acc[...] = product

    @pl.when(d > 0)
    def _():
        acc[...] += product

    @pl.when(d == pl.num_programs(1) - 1)
    def _():
        part = rows // QUARTERS
        at = pl.ds(pl.multiple_of(n * part, part), part)
        for t in range(FRAMES):
            for ref, who in ((own_ref, 1 - t), (send_ref, t)):

                @pl.when(ids_ref[4] == who)
                def _():
                    for quarter in range(QUARTERS):
                        lo = t * rows + quarter * part
                        ref[jnp.bitwise_xor(ids_ref[2], quarter), at, :] = (
                            acc[lo : lo + part] + acc[top + lo : top + lo + part]
                        )

        for ref, mine_too in ((own_ref, True), (send_ref, False)):

            @pl.when((ids_ref[3] == n) == mine_too)
            def _():
                for quarter in range(QUARTERS):
                    lo = 2 * rows + quarter * part
                    ref[jnp.bitwise_xor(ids_ref[2], quarter), 2 * part : 3 * part, :] = acc[lo : lo + part]

            for half in range(2):

                @pl.when(n == half)
                def _():
                    cover = acc[3 * rows : 3 * rows + 8]
                    for k in range(QUARTERS):
                        ref[k, 3 * part + half : 3 * part + 8, :] = cover[half:8]


def gram_products(order, ids, projector, measured):
    _, pixels, det = projector.shape
    rows = measured.shape[2]
    part = rows // QUARTERS
    shape = (QUARTERS, 3 * part + 8, pixels)
    out = pl.BlockSpec(shape, lambda n, d, o, s: (0, 0, 0))
    projector = pltpu.with_memory_space_constraint(projector, pltpu.HBM)
    measured = pltpu.with_memory_space_constraint(measured, pltpu.HBM)
    return pl.pallas_call(
        gram_kernel,
        out_shape=(jax.ShapeDtypeStruct(shape, F32),) * 2,
        grid_spec=pltpu.PrefetchScalarGridSpec(
            num_scalar_prefetch=2,
            grid=(2, det // CHUNK),
            in_specs=[
                pl.BlockSpec((None, pixels, CHUNK), lambda n, d, o, s: (o[n], 0, d)),
                pl.BlockSpec((None, None, rows, CHUNK), lambda n, d, o, s: (0, o[n], 0, d)),
                pl.BlockSpec((None, None, rows, CHUNK), lambda n, d, o, s: (1, o[n], 0, d)),
            ],
            out_specs=(out, out),
            scratch_shapes=[pltpu.VMEM((5 * rows + 16, pixels), F32)],
        ),
        compiler_params=params(24),
        name="gram_products",
    )(order, ids, projector, measured, measured)


def reduce_kernel(ids_ref, a0, a1, a2, a3, b_ref, gram_ref, aux_ref):
    part = gram_ref.shape[0]
    total = (a0[...] + a1[...]) + (a2[...] + a3[...])
    cov = total[3 * part : 3 * part + 8]
    scale = RELAXATION / cov
    share = cov / jnp.sum(cov, axis=1, keepdims=True)
    for n in range(2):
        b_ref[n] = total[n * part : (n + 1) * part] * scale[n : n + 1]
        aux_ref[n : n + 1] = RELAXATION * share[n : n + 1]
        aux_ref[2 + n : 3 + n] = scale[n : n + 1]
    rows = total[2 * part : 3 * part]
    own = jnp.sum(rows, axis=1, keepdims=True)
    mine = jnp.where(ids_ref[3] == 0, share[0:1], share[1:2])
    gram_ref[...] = (rows - own * mine).astype(BF16)


def place_gram_kernel(ids_ref, y0, y1, y2, y3, out_ref):
    z, y, h, tm = ids_ref[2], ids_ref[5], ids_ref[6], ids_ref[7]
    part = y0.shape[1]
    for dy, ref in enumerate((y0, y1, y2, y3)):
        for dx in range(4):
            slab = (
                jnp.bitwise_xor(tm, dx // 2) * 8
                + jnp.bitwise_xor(y, dy) * 2
                + jnp.bitwise_xor(h, dx % 2)
            )
            for k in range(QUARTERS):
                row = slab * (QUARTERS * part) + jnp.bitwise_xor(z, k) * part
                out_ref[pl.ds(pl.multiple_of(row, part), part), :] = ref[dx * QUARTERS + k]


def place_rows_kernel(ids_ref, z0, z1, z2, z3, out_ref):
    z = ids_ref[2]
    part = z0.shape[2]
    for k, ref in enumerate((z0, z1, z2, z3)):
        start = jnp.bitwise_xor(z, k) * part
        for slab in range(4):
            for n in range(2):
                row = slab * (QUARTERS * part) + start
                out_ref[n, pl.ds(pl.multiple_of(row, part), part), :] = ref[slab, n]


def tv_into(x_ref, g_ref, ss_ref, flux_ref, first, depth):
    height, pixels = x_ref.shape
    blocks = pixels // RY
    lane = lax.broadcasted_iota(jnp.int32, (height, RY), 1)
    zindex = first + lax.broadcasted_iota(jnp.int32, (height, RY), 0)
    inside = ((zindex >= 0) & (zindex < depth - 1)).astype(F32)
    column = (lane < RY - 1).astype(F32)
    flux_ref[...] = jnp.zeros_like(flux_ref)

    def block(i, folded):
        here_at = pl.ds(pl.multiple_of(i * RY, RY), RY)
        next_at = pl.ds(pl.multiple_of(jnp.minimum(i + 1, blocks - 1) * RY, RY), RY)
        here = x_ref[:, here_at]
        dz = (pltpu.roll(here, height - 1, 0) - here) * inside
        dc = (pltpu.roll(here, RY - 1, 1) - here) * column
        di = x_ref[:, next_at] - here
        square = dz * dz + dc * dc + di * di + SMOOTHING
        r = lax.rsqrt(square)
        r = r * (1.5 - 0.5 * square * r * r)
        fz = dz * r
        fc = dc * r
        fi = di * r
        g = (pltpu.roll(fz, 1, 0) - fz) + (flux_ref[...] - fi) + (pltpu.roll(fc, 1, 1) - fc)
        flux_ref[...] = fi
        g_ref[:, here_at] = g
        inner = g[HALO : height - HALO]
        piece = inner * inner
        for k in range(piece.shape[0] // 8):
            folded = folded + piece[8 * k : 8 * k + 8]
        return folded

    ss_ref[...] = lax.fori_loop(0, blocks, block, jnp.zeros((8, RY), F32))


def descend(x_ref, g_ref, sums, step, cells):
    folded = (sums[0][...] + sums[1][...]) + (sums[2][...] + sums[3][...])
    total = jnp.sum(folded, axis=(0, 1), keepdims=True)
    factor = (STEP_SCALE * STEP_DECAY**step) / jnp.sqrt(total / cells + NORM_GUARD)
    return x_ref[...] - factor * g_ref[...]


def first_kernel(ids_ref, x_ref, g_ref, ss_ref, flux, *, depth):
    tv_into(x_ref, g_ref, ss_ref, flux, ids_ref[0], depth)


def second_kernel(ids_ref, x_ref, g_ref, s0, s1, s2, s3, x_out, g_out, ss_out, flux, *, depth, step, cells):
    x_out[...] = descend(x_ref, g_ref, (s0, s1, s2, s3), step, cells)
    tv_into(x_out, g_out, ss_out, flux, ids_ref[0], depth)


def subset_kernel(
    ids_ref, x_ref, g_ref, s0, s1, s2, s3, mine_ref, other_ref, b_ref, aux_ref, *rest, depth, step, cells, final
):
    flux, product = rest[-2:]
    x_out = rest[0]
    x_out[...] = descend(x_ref, g_ref, (s0, s1, s2, s3), step, cells)
    core = ids_ref[3]

    def subset(n, carry):
        rounded = x_out[...].astype(BF16)

        @pl.when(n == core)
        def _():
            product[...] = jnp.dot(rounded, mine_ref[...], preferred_element_type=F32)

        @pl.when(n != core)
        def _():
            product[...] = jnp.dot(rounded, other_ref[...], preferred_element_type=F32)

        along = jnp.sum(rounded.astype(F32) * aux_ref[pl.ds(n, 1), :], axis=1, keepdims=True)
        change = b_ref[n] - product[...] * aux_ref[pl.ds(2 + n, 1), :] - along
        x_out[...] = jnp.maximum(x_out[...] + change, 0.0)
        return carry

    lax.fori_loop(0, 2, subset, 0)
    if not final:
        g_out, ss_out = rest[1:3]
        tv_into(x_out, g_out, ss_out, flux, ids_ref[0], depth)


def body(sinogram, projector, warm_volume, view_order):
    slices, pixels = warm_volume.shape
    part = slices // QUARTERS
    tm = lax.axis_index("tm").astype(jnp.int32)
    gz = lax.axis_index("gz").astype(jnp.int32)
    view = lax.axis_index("view").astype(jnp.int32)
    y, h = gz // 2, gz % 2
    z, c = view // 2, view % 2
    slab = tm * 8 + gz
    keeper = c == y // 2
    depth = slices * 16
    cells = depth * pixels
    inner = 4 * slices
    height = inner + 2 * HALO
    first = (2 * tm + c) * inner - HALO
    ids = jnp.stack([first, slab, z, c, keeper.astype(jnp.int32), y, h, tm])

    def pair_of(unit):
        across = move(unit, flip(dh=1), keeps)
        return jnp.where(h == 0, jnp.stack([unit, across]), jnp.stack([across, unit]))

    def strip_of(pair):
        one = move(pair, flip(dy=1), keeps)
        two = move(pair, flip(dy=2), keeps)
        three = move(pair, flip(dy=3), keeps)
        same = jnp.where(keeper, pair, two)
        flipped = jnp.where(keeper, one, three)
        return jnp.where(
            y % 2 == 0, jnp.concatenate([same, flipped]), jnp.concatenate([flipped, same])
        )

    def widen(array, dim):
        length = array.shape[dim]
        low = move(lax.slice_in_dim(array, length - HALO, length, axis=dim), strip_step(1))
        high = move(lax.slice_in_dim(array, 0, HALO, axis=dim), strip_step(-1))
        return jnp.concatenate([low, array, high], axis=dim)

    own, send = gram_products(view_order, ids, projector, sinogram)
    both = own + move(send, flip(dc=1))
    terms = [both[0]] + [move(both[k], flip(dz=k)) for k in range(1, QUARTERS)]
    b_unit, piece, aux = call(
        reduce_kernel,
        [((2, part, pixels), F32), ((part, pixels), BF16), ((8, pixels), F32)],
        ids,
        *terms,
    )

    line = jnp.stack([piece] + [move(piece, flip(dz=k)) for k in range(1, 4)])
    plane = jnp.concatenate(
        [line, move(line, flip(dh=1)), move(line, flip(dtm=1)), move(line, flip(dtm=1, dh=1))]
    )
    spread = [move(plane, flip(dy=k)) for k in range(1, 4)]

    def along_z(strip):
        return [strip] + [move(strip, flip(dz=k)) for k in range(1, 4)]

    def b_rows(quarters):
        (rows,) = call(place_rows_kernel, [((2, inner, pixels), F32)], ids, *quarters)
        return widen(rows, 1)

    strip = strip_of(pair_of(b_unit))
    quarters = along_z(strip)
    later = pair_of(move(after(b_unit, strip), flip(dc=1), lambda d: not keeps(d)))

    big = ((height, pixels), F32)
    small = ((8, RY), F32)
    flux = pltpu.VMEM((height, RY), F32)

    def everyone(sums):
        return [
            sums,
            move(sums, flip(dc=1)),
            move(sums, flip(dtm=1)),
            move(sums, flip(dtm=1, dc=1)),
        ]

    x = widen(strip_of(pair_of(after(warm_volume, both))).reshape(inner, pixels), 0)
    x = after(x, strip)
    g, sums = call(
        functools.partial(first_kernel, depth=depth), [big, small], ids, x, scratch=[flux]
    )
    b_wide = [None, None]
    finished = []
    for frame in range(FRAMES):
        for sweep in range(SWEEPS):
            step = sweep * TV_STEPS
            x, g, sums = call(
                functools.partial(second_kernel, depth=depth, step=step, cells=cells),
                [big, big, small],
                ids,
                x,
                g,
                *everyone(sums),
                scratch=[flux],
            )
            if frame == 0 and sweep == 0:
                (mine,) = call(
                    place_gram_kernel,
                    [((slices * 16, pixels), BF16)],
                    ids,
                    after(plane, sums),
                    *spread,
                )
                other = move(mine, flip(dc=1))
                b_wide[0] = b_rows(quarters)
            if frame == 0 and sweep == 1:
                later = along_z(after(later, x))
            if frame == 1 and sweep == 0:
                b_wide[1] = b_rows([after(later[0], x)] + later[1:])
            final = sweep == SWEEPS - 1 and frame == FRAMES - 1
            outs = call(
                functools.partial(subset_kernel, depth=depth, step=step + 1, cells=cells, final=final),
                [big] if final else [big, big, small],
                ids,
                x,
                g,
                *everyone(sums),
                mine,
                other,
                b_wide[frame],
                aux,
                scratch=[flux, pltpu.VMEM((height, pixels), F32)],
            )
            if final:
                x = outs[0]
            else:
                x, g, sums = outs
            if frame == 0 and sweep == 0:
                later = strip_of(after(later, x))
        start = HALO + (gz % 4) * slices
        local = lax.dynamic_slice_in_dim(x, start, slices, axis=0)
        passed = move(local, flip(dc=1), keeps)
        finished.append(jnp.where(keeper, local, passed))
    return jnp.stack(finished, axis=0)


def solution(mesh):
    return jax.shard_map(
        body,
        mesh=mesh,
        in_specs=(
            P(None, "view", ("tm", "gz"), None),
            P("view", None, None),
            P(("tm", "gz"), None),
            P(),
        ),
        out_specs=P(None, ("tm", "gz"), None),
        check_vma=False,
    )
```

```python
import functools

import jax
import jax.numpy as jnp
from jax import lax
from jax.experimental import pallas as pl
from jax.experimental.pallas import tpu as pltpu
from jax.sharding import PartitionSpec as P

RY = 128
FRAMES = 2
SWEEPS = 3
TV_STEPS = 2
HALO = 16
CHUNK = 512
QUARTERS = 4
AXES = ("tm", "gz", "view")

RELAXATION = 0.9
STEP_SCALE = 0.3
STEP_DECAY = 0.7
SMOOTHING = 0.01
NORM_GUARD = 1e-06

F32 = jnp.float32
BF16 = jnp.bfloat16
WHOLE = pl.BlockSpec(memory_space=pltpu.VMEM)
SCALARS = pl.BlockSpec(memory_space=pltpu.SMEM)


def params(mib):
    return pltpu.CompilerParams(vmem_limit_bytes=mib * 1024 * 1024)


def near(array):
    return pltpu.with_memory_space_constraint(array, pltpu.VMEM)


def call(kernel, outs, ids, *arrays, scratch=()):
    return pl.pallas_call(
        kernel,
        out_shape=tuple(pltpu.VMEM(shape, dtype) for shape, dtype in outs),
        in_specs=[SCALARS] + [WHOLE] * len(arrays),
        out_specs=tuple(WHOLE for _ in outs),
        scratch_shapes=scratch,
        compiler_params=params(12),
    )(ids, *[near(a) for a in arrays])


def keeps(d):
    return d[4] == d[1] // 2


def move(array, rule, source=None):
    pairs = []
    for tm in range(2):
        for y in range(4):
            for h in range(2):
                for z in range(4):
                    for c in range(2):
                        here = (tm, y, h, z, c)
                        if source is not None and not source(here):
                            continue
                        there = rule(*here)
                        if there is None:
                            continue
                        index = [((t * 4 + a) * 2 + b) * 8 + 2 * u + v for t, a, b, u, v in (here, there)]
                        pairs.append(tuple(index))
    return lax.ppermute(array, AXES, pairs)


def after(array, *others):
    return lax.optimization_barrier((array, *others))[0]


def flip(dtm=0, dy=0, dh=0, dz=0, dc=0):
    return lambda tm, y, h, z, c: (tm ^ dtm, y ^ dy, h ^ dh, z ^ dz, c ^ dc)


def strip_step(step):
    def rule(tm, y, h, z, c):
        strip = 2 * tm + c + step
        return (strip // 2, y, h, z, strip % 2) if 0 <= strip < 4 else None

    return rule


def gram_kernel(order_ref, ids_ref, a_ref, s0_ref, s1_ref, own_ref, send_ref, acc, level_ref):
    n = pl.program_id(0)
    d = pl.program_id(1)
    rows = s0_ref.shape[0]
    tile = a_ref[...]
    ray = jnp.sum(tile.astype(F32), axis=0, keepdims=True)
    inverse = 1.0 / ray
    lhs = []
    for t, ref in enumerate((s0_ref, s1_ref)):
        scaled = ref[...].astype(F32) * inverse

        @pl.when(d == 0)
        def _():
            mean = jnp.sum(scaled, axis=1, keepdims=True) / CHUNK
            level_ref[t] = jnp.broadcast_to(mean, level_ref.shape[1:])

        lhs.append((scaled - level_ref[t, :, 0:1]).astype(BF16))
    mine = a_ref[pl.ds(pl.multiple_of(ids_ref[1] * rows, rows), rows), :]
    lhs.append((mine.astype(F32) * inverse).astype(BF16))
    lhs.append(jnp.ones((16, CHUNK), BF16))
    stack = jnp.concatenate(lhs, axis=0)
    product = lax.dot_general(stack, tile, (((1,), (1,)), ((), ())), preferred_element_type=F32)

    @pl.when(d == 0)
    def _():
        acc[...] = product

    @pl.when(d > 0)
    def _():
        acc[...] += product

    @pl.when(d == pl.num_programs(1) - 1)
    def _():
        part = rows // QUARTERS
        at = pl.ds(pl.multiple_of(n * part, part), part)
        for t in range(FRAMES):
            for ref, who in ((own_ref, 1 - t), (send_ref, t)):

                @pl.when(ids_ref[4] == who)
                def _():
                    for quarter in range(QUARTERS):
                        lo = quarter * part
                        ref[jnp.bitwise_xor(ids_ref[2], quarter), at, :] = (
                            acc[t * rows + lo : t * rows + lo + part]
                            + level_ref[t, lo : lo + part, 0:1] * acc[3 * rows : 3 * rows + 1]
                        )

        for ref, mine_too in ((own_ref, True), (send_ref, False)):

            @pl.when((ids_ref[3] == n) == mine_too)
            def _():
                for quarter in range(QUARTERS):
                    lo = 2 * rows + quarter * part
                    ref[jnp.bitwise_xor(ids_ref[2], quarter), 2 * part : 3 * part, :] = acc[lo : lo + part]

            for half in range(2):

                @pl.when(n == half)
                def _():
                    cover = acc[3 * rows : 3 * rows + 8]
                    for k in range(QUARTERS):
                        ref[k, 3 * part + half : 3 * part + 8, :] = cover[half:8]


def gram_products(order, ids, projector, measured):
    _, pixels, det = projector.shape
    rows = measured.shape[2]
    part = rows // QUARTERS
    shape = (QUARTERS, 3 * part + 8, pixels)
    out = pl.BlockSpec(shape, lambda n, d, o, s: (0, 0, 0))
    projector = pltpu.with_memory_space_constraint(projector, pltpu.HBM)
    measured = pltpu.with_memory_space_constraint(measured, pltpu.HBM)
    return pl.pallas_call(
        gram_kernel,
        out_shape=(jax.ShapeDtypeStruct(shape, F32),) * 2,
        grid_spec=pltpu.PrefetchScalarGridSpec(
            num_scalar_prefetch=2,
            grid=(2, det // CHUNK),
            in_specs=[
                pl.BlockSpec((None, pixels, CHUNK), lambda n, d, o, s: (o[n], 0, d)),
                pl.BlockSpec((None, None, rows, CHUNK), lambda n, d, o, s: (0, o[n], 0, d)),
                pl.BlockSpec((None, None, rows, CHUNK), lambda n, d, o, s: (1, o[n], 0, d)),
            ],
            out_specs=(out, out),
            scratch_shapes=[pltpu.VMEM((3 * rows + 16, pixels), F32), pltpu.VMEM((FRAMES, rows, RY), F32)],
        ),
        compiler_params=params(24),
        name="gram_products",
    )(order, ids, projector, measured, measured)


def reduce_kernel(ids_ref, a0, a1, a2, a3, b_ref, gram_ref, aux_ref):
    part = gram_ref.shape[0]
    total = (a0[...] + a1[...]) + (a2[...] + a3[...])
    cov = total[3 * part : 3 * part + 8]
    scale = RELAXATION / cov
    share = cov / jnp.sum(cov, axis=1, keepdims=True)
    for n in range(2):
        b_ref[n] = total[n * part : (n + 1) * part] * scale[n : n + 1]
        aux_ref[n : n + 1] = RELAXATION * share[n : n + 1]
        aux_ref[2 + n : 3 + n] = scale[n : n + 1]
    rows = total[2 * part : 3 * part]
    own = jnp.sum(rows, axis=1, keepdims=True)
    mine = jnp.where(ids_ref[3] == 0, share[0:1], share[1:2])
    gram_ref[...] = (rows - own * mine).astype(BF16)


def place_gram_kernel(ids_ref, y0, y1, y2, y3, out_ref):
    z, y, h, tm = ids_ref[2], ids_ref[5], ids_ref[6], ids_ref[7]
    part = y0.shape[1]
    for dy, ref in enumerate((y0, y1, y2, y3)):
        for dx in range(4):
            slab = (
                jnp.bitwise_xor(tm, dx // 2) * 8
                + jnp.bitwise_xor(y, dy) * 2
                + jnp.bitwise_xor(h, dx % 2)
            )
            for k in range(QUARTERS):
                row = slab * (QUARTERS * part) + jnp.bitwise_xor(z, k) * part
                out_ref[pl.ds(pl.multiple_of(row, part), part), :] = ref[dx * QUARTERS + k]


def place_rows_kernel(ids_ref, z0, z1, z2, z3, out_ref):
    z = ids_ref[2]
    part = z0.shape[2]
    for k, ref in enumerate((z0, z1, z2, z3)):
        start = jnp.bitwise_xor(z, k) * part
        for slab in range(4):
            for n in range(2):
                row = slab * (QUARTERS * part) + start
                out_ref[n, pl.ds(pl.multiple_of(row, part), part), :] = ref[slab, n]


def tv_into(x_ref, g_ref, ss_ref, flux_ref, first, depth):
    height, pixels = x_ref.shape
    blocks = pixels // RY
    lane = lax.broadcasted_iota(jnp.int32, (height, RY), 1)

    @pl.when(first < 0)
    def _():
        x_ref[HALO - 1 : HALO, :] = x_ref[HALO : HALO + 1, :]

    @pl.when(first + height > depth)
    def _():
        x_ref[height - HALO : height - HALO + 1, :] = x_ref[height - HALO - 1 : height - HALO, :]

    column = (lane < RY - 1).astype(F32)
    flux_ref[...] = jnp.zeros_like(flux_ref)

    def block(i, folded):
        here_at = pl.ds(pl.multiple_of(i * RY, RY), RY)
        next_at = pl.ds(pl.multiple_of(jnp.minimum(i + 1, blocks - 1) * RY, RY), RY)
        here = x_ref[:, here_at]
        dz = pltpu.roll(here, height - 1, 0) - here
        dc = (pltpu.roll(here, RY - 1, 1) - here) * column
        di = x_ref[:, next_at] - here
        square = dz * dz + dc * dc + di * di + SMOOTHING
        r = lax.rsqrt(square)
        r = r * (1.5 - (0.5 * square) * (r * r))
        fz = dz * r
        fc = dc * r
        fi = di * r
        g = (pltpu.roll(fz, 1, 0) - fz) + (flux_ref[...] - fi) + (pltpu.roll(fc, 1, 1) - fc)
        flux_ref[...] = fi
        g_ref[:, here_at] = g
        inner = g[HALO : height - HALO]
        piece = inner * inner
        for k in range(piece.shape[0] // 8):
            folded = folded + piece[8 * k : 8 * k + 8]
        return folded

    ss_ref[...] = lax.fori_loop(0, blocks, block, jnp.zeros((8, RY), F32))


def descend(x_ref, g_ref, sums, step, cells):
    folded = (sums[0][...] + sums[1][...]) + (sums[2][...] + sums[3][...])
    total = jnp.sum(folded, axis=(0, 1), keepdims=True)
    factor = (STEP_SCALE * STEP_DECAY**step) / jnp.sqrt(total / cells + NORM_GUARD)
    return x_ref[...] - factor * g_ref[...]


def first_kernel(ids_ref, x_ref, x_out, g_ref, ss_ref, flux, *, depth):
    x_out[...] = x_ref[...]
    tv_into(x_out, g_ref, ss_ref, flux, ids_ref[0], depth)


def second_kernel(ids_ref, x_ref, g_ref, s0, s1, s2, s3, x_out, g_out, ss_out, flux, *, depth, step, cells):
    x_out[...] = descend(x_ref, g_ref, (s0, s1, s2, s3), step, cells)
    tv_into(x_out, g_out, ss_out, flux, ids_ref[0], depth)


def subset_kernel(
    ids_ref, x_ref, g_ref, s0, s1, s2, s3, mine_ref, other_ref, b_ref, aux_ref, *rest, depth, step, cells, final
):
    flux, product = rest[-2:]
    x_out = rest[0]
    x_out[...] = descend(x_ref, g_ref, (s0, s1, s2, s3), step, cells)
    core = ids_ref[3]

    def subset(n, carry):
        rounded = x_out[...].astype(BF16)

        @pl.when(n == core)
        def _():
            product[...] = jnp.dot(rounded, mine_ref[...], preferred_element_type=F32)

        @pl.when(n != core)
        def _():
            product[...] = jnp.dot(rounded, other_ref[...], preferred_element_type=F32)

        along = jnp.sum(rounded.astype(F32) * aux_ref[pl.ds(n, 1), :], axis=1, keepdims=True)
        change = b_ref[n] - product[...] * aux_ref[pl.ds(2 + n, 1), :] - along
        x_out[...] = jnp.maximum(x_out[...] + change, 0.0)
        return carry

    lax.fori_loop(0, 2, subset, 0)
    if not final:
        g_out, ss_out = rest[1:3]
        tv_into(x_out, g_out, ss_out, flux, ids_ref[0], depth)


def body(sinogram, projector, warm_volume, view_order):
    slices, pixels = warm_volume.shape
    part = slices // QUARTERS
    tm = lax.axis_index("tm").astype(jnp.int32)
    gz = lax.axis_index("gz").astype(jnp.int32)
    view = lax.axis_index("view").astype(jnp.int32)
    y, h = gz // 2, gz % 2
    z, c = view // 2, view % 2
    slab = tm * 8 + gz
    keeper = c == y // 2
    depth = slices * 16
    cells = depth * pixels
    inner = 4 * slices
    height = inner + 2 * HALO
    first = (2 * tm + c) * inner - HALO
    ids = jnp.stack([first, slab, z, c, keeper.astype(jnp.int32), y, h, tm])

    def pair_of(unit):
        across = move(unit, flip(dh=1), keeps)
        return jnp.where(h == 0, jnp.stack([unit, across]), jnp.stack([across, unit]))

    def strip_of(pair):
        one, two, three = (move(pair, flip(dy=k), keeps) for k in range(1, 4))
        same = jnp.where(keeper, pair, two)
        flipped = jnp.where(keeper, one, three)
        return jnp.where(
            y % 2 == 0, jnp.concatenate([same, flipped]), jnp.concatenate([flipped, same])
        )

    def widen(array, dim):
        length = array.shape[dim]
        low = move(lax.slice_in_dim(array, length - HALO, length, axis=dim), strip_step(1))
        high = move(lax.slice_in_dim(array, 0, HALO, axis=dim), strip_step(-1))
        return jnp.concatenate([low, array, high], axis=dim)

    warm_pair = pair_of(warm_volume)
    own, send = gram_products(view_order, ids, projector, sinogram)
    both = own + move(send, flip(dc=1))
    terms = [both[0]] + [move(both[k], flip(dz=k)) for k in range(1, QUARTERS)]
    b_unit, piece, aux = call(
        reduce_kernel, [((2, part, pixels), F32), ((part, pixels), BF16), ((8, pixels), F32)], ids, *terms
    )

    line = jnp.stack([piece] + [move(piece, flip(dz=k)) for k in range(1, 4)])
    flips = (flip(dh=1), flip(dtm=1), flip(dtm=1, dh=1))
    plane = jnp.concatenate([line] + [move(line, f) for f in flips])
    spread = [move(plane, flip(dy=k)) for k in range(1, 4)]

    def along_z(strip):
        return [strip] + [move(strip, flip(dz=k)) for k in range(1, 4)]

    def b_rows(quarters):
        (rows,) = call(place_rows_kernel, [((2, inner, pixels), F32)], ids, *quarters)
        return widen(rows, 1)

    strip = strip_of(pair_of(b_unit))
    quarters = along_z(strip)
    later = move(after(b_unit, strip), flip(dc=1), lambda d: not keeps(d))
    later = along_z(strip_of(pair_of(later)))

    big = ((height, pixels), F32)
    small = ((8, RY), F32)
    flux = pltpu.VMEM((height, RY), F32)

    def everyone(sums):
        return [
            sums,
            move(sums, flip(dc=1)),
            move(sums, flip(dtm=1)),
            move(sums, flip(dtm=1, dc=1)),
        ]

    x = widen(strip_of(after(warm_pair, both)).reshape(inner, pixels), 0)
    x = after(x, strip)
    x, g, sums = call(functools.partial(first_kernel, depth=depth), [big, big, small], ids, x, scratch=[flux])
    b_wide = [None, None]
    finished = []
    for frame in range(FRAMES):
        for sweep in range(SWEEPS):
            step = sweep * TV_STEPS
            x, g, sums = call(
                functools.partial(second_kernel, depth=depth, step=step, cells=cells),
                [big, big, small],
                ids,
                x,
                g,
                *everyone(sums),
                scratch=[flux],
            )
            if frame == 0 and sweep == 0:
                (mine,) = call(place_gram_kernel, [((slices * 16, pixels), BF16)], ids, after(plane, sums), *spread)
                other = move(mine, flip(dc=1))
                b_wide[0] = b_rows(quarters)
            if frame == 0 and sweep == 2:
                b_wide[1] = b_rows([after(later[0], x)] + later[1:])
            final = sweep == SWEEPS - 1 and frame == FRAMES - 1
            outs = call(
                functools.partial(subset_kernel, depth=depth, step=step + 1, cells=cells, final=final),
                [big] if final else [big, big, small],
                ids,
                x,
                g,
                *everyone(sums),
                mine,
                other,
                b_wide[frame],
                aux,
                scratch=[flux, pltpu.VMEM((height, pixels), F32)],
            )
            if final:
                x = outs[0]
            else:
                x, g, sums = outs
        start = HALO + (gz % 4) * slices
        local = lax.dynamic_slice_in_dim(x, start, slices, axis=0)
        passed = move(local, flip(dc=1), keeps)
        finished.append(jnp.where(keeper, local, passed))
    return jnp.stack(finished, axis=0)


def solution(mesh):
    return jax.shard_map(
        body,
        mesh=mesh,
        in_specs=(
            P(None, "view", ("tm", "gz"), None),
            P("view", None, None),
            P(("tm", "gz"), None),
            P(),
        ),
        out_specs=P(None, ("tm", "gz"), None),
        check_vma=False,
    )
```

```python
import functools

import jax
import jax.numpy as jnp
from jax import lax
from jax.experimental import pallas as pl
from jax.experimental.pallas import tpu as pltpu
from jax.sharding import PartitionSpec as P

RY = 128
FRAMES = 2
SWEEPS = 3
TV_STEPS = 2
HALO = 16
CHUNK = 1280
ROWS = 32
QUARTERS = 4
AXES = ("tm", "gz", "view")

RELAXATION = 0.9
STEP_SCALE = 0.3
STEP_DECAY = 0.7
SMOOTHING = 0.01
NORM_GUARD = 1e-06

F32 = jnp.float32
BF16 = jnp.bfloat16
WHOLE = pl.BlockSpec(memory_space=pltpu.VMEM)
SCALARS = pl.BlockSpec(memory_space=pltpu.SMEM)


def params(mib):
    return pltpu.CompilerParams(vmem_limit_bytes=mib * 1024 * 1024)


def near(array):
    return pltpu.with_memory_space_constraint(array, pltpu.VMEM)


def call(kernel, outs, ids, *arrays, scratch=()):
    return pl.pallas_call(
        kernel,
        out_shape=tuple(pltpu.VMEM(shape, dtype) for shape, dtype in outs),
        in_specs=[SCALARS] + [WHOLE] * len(arrays),
        out_specs=tuple(WHOLE for _ in outs),
        scratch_shapes=scratch,
        compiler_params=params(12),
    )(ids, *[near(a) for a in arrays])


def keeps(d):
    return d[4] == d[1] // 2


def move(array, rule, source=None):
    pairs = []
    for tm in range(2):
        for y in range(4):
            for h in range(2):
                for z in range(4):
                    for c in range(2):
                        here = (tm, y, h, z, c)
                        if source is not None and not source(here):
                            continue
                        there = rule(*here)
                        if there is None:
                            continue
                        index = [((t * 4 + a) * 2 + b) * 8 + 2 * u + v for t, a, b, u, v in (here, there)]
                        pairs.append(tuple(index))
    return lax.ppermute(array, AXES, pairs)


def after(array, *others):
    return lax.optimization_barrier((array, *others))[0]


def flip(dtm=0, dy=0, dh=0, dz=0, dc=0):
    return lambda tm, y, h, z, c: (tm ^ dtm, y ^ dy, h ^ dh, z ^ dz, c ^ dc)


def strip_step(step):
    def rule(tm, y, h, z, c):
        strip = 2 * tm + c + step
        return (strip // 2, y, h, z, strip % 2) if 0 <= strip < 4 else None

    return rule


def gram_kernel(order_ref, ids_ref, a_ref, s0_ref, s1_ref, own_ref, send_ref, acc, level_ref):
    n = pl.program_id(0)
    rows, det = s0_ref.shape
    my_rows = pl.ds(pl.multiple_of(ids_ref[1] * rows, rows), rows)

    def chunk(d, first):
        at = pl.ds(d * CHUNK, CHUNK) if first else pl.ds(pl.multiple_of(d * CHUNK, CHUNK), CHUNK)
        tile = a_ref[:, at]
        ray = jnp.sum(tile.astype(F32), axis=0, keepdims=True)
        inverse = 1.0 / ray
        lhs = []
        for t, ref in enumerate((s0_ref, s1_ref)):
            scaled = ref[:, at].astype(F32) * inverse
            if first:
                mean = jnp.sum(scaled, axis=1, keepdims=True) / CHUNK
                level_ref[t] = jnp.broadcast_to(mean, level_ref.shape[1:])
            lhs.append((scaled - level_ref[t, :, 0:1]).astype(BF16))
        lhs.append((a_ref[my_rows, at].astype(F32) * inverse).astype(BF16))
        lhs.append(jnp.ones((16, CHUNK), BF16))
        stack = jnp.concatenate(lhs, axis=0)
        product = lax.dot_general(stack, tile, (((1,), (1,)), ((), ())), preferred_element_type=F32)
        if first:
            acc[...] = product
        else:
            acc[...] += product

    chunk(0, True)

    def further(d, carry):
        chunk(d, False)
        return carry

    lax.fori_loop(1, det // CHUNK, further, 0)

    part = rows // QUARTERS
    at = pl.ds(pl.multiple_of(n * part, part), part)
    for t in range(FRAMES):
        for ref, who in ((own_ref, 1 - t), (send_ref, t)):

            @pl.when(ids_ref[4] == who)
            def _():
                for quarter in range(QUARTERS):
                    lo = quarter * part
                    ref[jnp.bitwise_xor(ids_ref[2], quarter), at, :] = (
                        acc[t * rows + lo : t * rows + lo + part]
                        + level_ref[t, lo : lo + part, 0:1] * acc[3 * rows : 3 * rows + 1]
                    )

    for ref, mine_too in ((own_ref, True), (send_ref, False)):

        @pl.when((ids_ref[3] == n) == mine_too)
        def _():
            for quarter in range(QUARTERS):
                lo = 2 * rows + quarter * part
                ref[jnp.bitwise_xor(ids_ref[2], quarter), 2 * part : 3 * part, :] = acc[lo : lo + part]

        for half in range(2):

            @pl.when(n == half)
            def _():
                cover = acc[3 * rows : 3 * rows + 8]
                for k in range(QUARTERS):
                    ref[k, 3 * part + half : 3 * part + 8, :] = cover[half:8]


def gram_products(order, ids, projector, measured):
    _, pixels, det = projector.shape
    rows = measured.shape[2]
    part = rows // QUARTERS
    shape = (QUARTERS, 3 * part + 8, pixels)
    out = pl.BlockSpec(shape, lambda n, o, s: (0, 0, 0))
    projector = pltpu.with_memory_space_constraint(projector, pltpu.HBM)
    measured = pltpu.with_memory_space_constraint(measured, pltpu.HBM)
    return pl.pallas_call(
        gram_kernel,
        out_shape=(jax.ShapeDtypeStruct(shape, F32),) * 2,
        grid_spec=pltpu.PrefetchScalarGridSpec(
            num_scalar_prefetch=2,
            grid=(2,),
            in_specs=[
                pl.BlockSpec((None, pixels, det), lambda n, o, s: (o[n], 0, 0)),
                pl.BlockSpec((None, None, rows, det), lambda n, o, s: (0, o[n], 0, 0)),
                pl.BlockSpec((None, None, rows, det), lambda n, o, s: (1, o[n], 0, 0)),
            ],
            out_specs=(out, out),
            scratch_shapes=[pltpu.VMEM((3 * rows + 16, pixels), F32), pltpu.VMEM((FRAMES, rows, RY), F32)],
        ),
        compiler_params=params(24),
        name="gram_products",
    )(order, ids, projector, measured, measured)


def chip_sum_kernel(ids_ref, own_ref, got_ref, *outs):
    for k, out in enumerate(outs):
        out[...] = own_ref[k] + got_ref[k]


def reduce_kernel(ids_ref, a0, a1, a2, a3, b_ref, gram_ref, aux_ref):
    part = gram_ref.shape[0]
    total = (a0[...] + a1[...]) + (a2[...] + a3[...])
    cov = total[3 * part : 3 * part + 8]
    scale = RELAXATION / cov
    share = cov / jnp.sum(cov, axis=1, keepdims=True)
    for n in range(2):
        b_ref[n] = total[n * part : (n + 1) * part] * scale[n : n + 1]
        aux_ref[n : n + 1] = RELAXATION * share[n : n + 1]
        aux_ref[2 + n : 3 + n] = scale[n : n + 1]
    rows = total[2 * part : 3 * part]
    own = jnp.sum(rows, axis=1, keepdims=True)
    mine = jnp.where(ids_ref[3] == 0, share[0:1], share[1:2])
    gram_ref[...] = (rows - own * mine).astype(BF16)


def place_gram_kernel(ids_ref, y0, y1, y2, y3, out_ref):
    z, y, h, tm = ids_ref[2], ids_ref[5], ids_ref[6], ids_ref[7]
    part = y0.shape[1]
    for dy, ref in enumerate((y0, y1, y2, y3)):
        for dx in range(4):
            slab = (
                jnp.bitwise_xor(tm, dx // 2) * 8
                + jnp.bitwise_xor(y, dy) * 2
                + jnp.bitwise_xor(h, dx % 2)
            )
            for k in range(QUARTERS):
                row = slab * (QUARTERS * part) + jnp.bitwise_xor(z, k) * part
                out_ref[pl.ds(pl.multiple_of(row, part), part), :] = ref[dx * QUARTERS + k]


def place_rows_kernel(ids_ref, z0, z1, z2, z3, out_ref, head_ref, tail_ref):
    z = ids_ref[2]
    part = z0.shape[2]
    for k, ref in enumerate((z0, z1, z2, z3)):
        start = jnp.bitwise_xor(z, k) * part
        for slab in range(4):
            for n in range(2):
                row = slab * (QUARTERS * part) + start
                out_ref[n, pl.ds(pl.multiple_of(row, part), part), :] = ref[slab, n]
    head_ref[...] = out_ref[:, :HALO]
    tail_ref[...] = out_ref[:, out_ref.shape[1] - HALO :]


def tv_into(x_ref, g_ref, ss_ref, flux_ref, first, depth):
    height, pixels = x_ref.shape
    blocks = pixels // RY

    @pl.when(first < 0)
    def _():
        x_ref[HALO - 1 : HALO, :] = x_ref[HALO : HALO + 1, :]

    @pl.when(first + height > depth)
    def _():
        x_ref[height - HALO : height - HALO + 1, :] = x_ref[height - HALO - 1 : height - HALO, :]

    column = (lax.broadcasted_iota(jnp.int32, (ROWS, RY), 1) < RY - 1).astype(F32)
    flux_ref[...] = jnp.zeros_like(flux_ref)

    def block(i, folded):
        here_at = pl.ds(pl.multiple_of(i * RY, RY), RY)
        next_at = pl.ds(pl.multiple_of(jnp.minimum(i + 1, blocks - 1) * RY, RY), RY)
        above = jnp.zeros((8, RY), F32)
        for lo in range(0, height, ROWS):
            hi = lo + ROWS
            here = x_ref[lo:hi, here_at]
            tail = x_ref[hi : hi + 8, here_at] if hi < height else here[ROWS - 8 :]
            below = pltpu.roll(jnp.concatenate([here, tail]), ROWS + 7, 0)[:ROWS]
            dz = below - here
            dc = (pltpu.roll(here, RY - 1, 1) - here) * column
            di = x_ref[lo:hi, next_at] - here
            square = dz * dz + dc * dc + di * di + SMOOTHING
            r = lax.rsqrt(square)
            r = r * (1.5 - (0.5 * square) * (r * r))
            fz = dz * r
            fc = dc * r
            fi = di * r
            over = pltpu.roll(jnp.concatenate([above, fz]), 1, 0)[8:]
            above = fz[ROWS - 8 :]
            g = (over - fz) + (flux_ref[lo:hi] - fi) + (pltpu.roll(fc, 1, 1) - fc)
            flux_ref[lo:hi] = fi
            g_ref[lo:hi, here_at] = g
            for k in range(0, ROWS, 8):
                if HALO <= lo + k < height - HALO:
                    folded = folded + g[k : k + 8] * g[k : k + 8]
        return folded

    ss_ref[...] = lax.fori_loop(0, blocks, block, jnp.zeros((8, RY), F32))


def descend(x_ref, g_ref, sums, step, cells):
    folded = (sums[0][...] + sums[1][...]) + (sums[2][...] + sums[3][...])
    total = jnp.sum(folded, axis=(0, 1), keepdims=True)
    factor = (STEP_SCALE * STEP_DECAY**step) / jnp.sqrt(total / cells + NORM_GUARD)
    return x_ref[...] - factor * g_ref[...]


def first_kernel(ids_ref, x_ref, x_out, g_ref, ss_ref, flux, *, depth):
    x_out[...] = x_ref[...]
    tv_into(x_out, g_ref, ss_ref, flux, ids_ref[0], depth)


def second_kernel(ids_ref, x_ref, g_ref, s0, s1, s2, s3, x_out, g_out, ss_out, flux, *, depth, step, cells):
    x_out[...] = descend(x_ref, g_ref, (s0, s1, s2, s3), step, cells)
    tv_into(x_out, g_out, ss_out, flux, ids_ref[0], depth)


def subset_kernel(
    ids_ref, x_ref, g_ref, s0, s1, s2, s3, mine_ref, other_ref, low_ref, b_ref, high_ref, aux_ref, *rest, depth, step, cells, last, final
):
    flux, product = rest[-2:]
    x_out = rest[0]
    height = x_ref.shape[0]
    parts = ((low_ref, 0, HALO), (b_ref, HALO, height - HALO), (high_ref, height - HALO, height))
    x_out[...] = descend(x_ref, g_ref, (s0, s1, s2, s3), step, cells)
    core = ids_ref[3]

    def subset(n, carry):
        rounded = x_out[...].astype(BF16)

        @pl.when(n == core)
        def _():
            product[...] = jnp.dot(rounded, mine_ref[...], preferred_element_type=F32)

        @pl.when(n != core)
        def _():
            product[...] = jnp.dot(rounded, other_ref[...], preferred_element_type=F32)

        along = jnp.sum(rounded.astype(F32) * aux_ref[pl.ds(n, 1), :], axis=1, keepdims=True)
        scale = aux_ref[pl.ds(2 + n, 1), :]
        for ref, lo, hi in parts:
            change = ref[n] - product[lo:hi] * scale - along[lo:hi]
            x_out[lo:hi] = jnp.maximum(x_out[lo:hi] + change, 0.0)
        return carry

    lax.fori_loop(0, 2, subset, 0)
    if last:
        slab_out = rest[1]
        rows = slab_out.shape[0]
        start = HALO + jnp.bitwise_and(ids_ref[1], 3) * rows
        slab_out[...] = x_out[pl.ds(pl.multiple_of(start, HALO), rows), :]
    if not final:
        g_out, ss_out = rest[1 + last : 3 + last]
        tv_into(x_out, g_out, ss_out, flux, ids_ref[0], depth)


def body(sinogram, projector, warm_volume, view_order):
    slices, pixels = warm_volume.shape
    part = slices // QUARTERS
    tm = lax.axis_index("tm").astype(jnp.int32)
    gz = lax.axis_index("gz").astype(jnp.int32)
    view = lax.axis_index("view").astype(jnp.int32)
    y, h = gz // 2, gz % 2
    z, c = view // 2, view % 2
    slab = tm * 8 + gz
    keeper = c == y // 2
    depth = slices * 16
    cells = depth * pixels
    inner = 4 * slices
    height = inner + 2 * HALO
    first = (2 * tm + c) * inner - HALO
    ids = jnp.stack([first, slab, z, c, keeper.astype(jnp.int32), y, h, tm])

    def pair_of(unit):
        across = move(unit, flip(dh=1), keeps)
        return jnp.where(h == 0, jnp.stack([unit, across]), jnp.stack([across, unit]))

    def strip_of(pair):
        one, two, three = (move(pair, flip(dy=k), keeps) for k in range(1, 4))
        same = jnp.where(keeper, pair, two)
        flipped = jnp.where(keeper, one, three)
        return jnp.where(
            y % 2 == 0, jnp.concatenate([same, flipped]), jnp.concatenate([flipped, same])
        )

    def widen(array, dim):
        length = array.shape[dim]
        low = move(lax.slice_in_dim(array, length - HALO, length, axis=dim), strip_step(1))
        high = move(lax.slice_in_dim(array, 0, HALO, axis=dim), strip_step(-1))
        return jnp.concatenate([low, array, high], axis=dim)

    own, send = gram_products(view_order, ids, projector, sinogram)
    passed = move(send, flip(dc=1))
    warm_pair = pair_of(after(warm_volume, send))
    block = (own.shape[1:], F32)
    terms = call(chip_sum_kernel, [block] * QUARTERS, ids, own, passed)
    terms = [terms[0]] + [move(terms[k], flip(dz=k)) for k in range(1, QUARTERS)]
    b_unit, piece, aux = call(
        reduce_kernel,
        [((2, part, pixels), F32), ((part, pixels), BF16), ((8, pixels), F32)],
        ids,
        *terms,
    )

    line = jnp.stack([piece] + [move(piece, flip(dz=k)) for k in range(1, 4)])
    flips = (flip(dh=1), flip(dtm=1), flip(dtm=1, dh=1))
    plane = jnp.concatenate([line] + [move(line, f) for f in flips])
    spread = [move(plane, flip(dy=k)) for k in range(1, 4)]

    def along_z(strip):
        return [strip] + [move(strip, flip(dz=k)) for k in range(1, 4)]

    def b_rows(quarters):
        edge = ((2, HALO, pixels), F32)
        rows, head, tail = call(
            place_rows_kernel, [((2, inner, pixels), F32), edge, edge], ids, *quarters
        )
        return move(tail, strip_step(1)), rows, move(head, strip_step(-1))

    strip = strip_of(pair_of(b_unit))
    quarters = along_z(strip)
    later = move(after(b_unit, strip), flip(dc=1), lambda d: not keeps(d))
    later = along_z(strip_of(pair_of(later)))

    big = ((height, pixels), F32)
    small = ((8, RY), F32)
    flux = pltpu.VMEM((height, RY), F32)

    def everyone(sums):
        return [
            sums,
            move(sums, flip(dc=1)),
            move(sums, flip(dtm=1)),
            move(sums, flip(dtm=1, dc=1)),
        ]

    x = widen(strip_of(after(warm_pair, terms[0])).reshape(inner, pixels), 0)
    x = after(x, strip)
    x, g, sums = call(
        functools.partial(first_kernel, depth=depth), [big, big, small], ids, x, scratch=[flux]
    )
    b_wide = [None, None]
    finished = []
    for frame in range(FRAMES):
        for sweep in range(SWEEPS):
            step = sweep * TV_STEPS
            x, g, sums = call(
                functools.partial(second_kernel, depth=depth, step=step, cells=cells),
                [big, big, small],
                ids,
                x,
                g,
                *everyone(sums),
                scratch=[flux],
            )
            if frame == 0 and sweep == 0:
                (mine,) = call(
                    place_gram_kernel,
                    [((slices * 16, pixels), BF16)],
                    ids,
                    after(plane, sums),
                    *spread,
                )
                other = move(mine, flip(dc=1))
                b_wide[0] = b_rows(quarters)
            if frame == 0 and sweep == 2:
                b_wide[1] = b_rows([after(later[0], x)] + later[1:])
            last = sweep == SWEEPS - 1
            final = last and frame == FRAMES - 1
            outs = [big] + [((slices, pixels), F32)] * last
            if not final:
                outs += [big, small]
            outs = call(
                functools.partial(
                    subset_kernel, depth=depth, step=step + 1, cells=cells, last=last, final=final
                ),
                outs,
                ids,
                x,
                g,
                *everyone(sums),
                mine,
                other,
                *b_wide[frame],
                aux,
                scratch=[flux, pltpu.VMEM((height, pixels), F32)],
            )
            x = outs[0]
            if not final:
                g, sums = outs[-2:]
        local = outs[1]
        passed = move(local, flip(dc=1), keeps)
        finished.append(jnp.where(keeper, local, passed))
    return jnp.stack(finished, axis=0)


def solution(mesh):
    return jax.shard_map(
        body,
        mesh=mesh,
        in_specs=(
            P(None, "view", ("tm", "gz"), None),
            P("view", None, None),
            P(("tm", "gz"), None),
            P(),
        ),
        out_specs=P(None, ("tm", "gz"), None),
        check_vma=False,
    )
```

```python
import functools

import jax
import jax.numpy as jnp
from jax import lax
from jax.experimental import pallas as pl
from jax.experimental.pallas import tpu as pltpu
from jax.sharding import PartitionSpec as P

RY = 128
FRAMES = 2
SWEEPS = 3
TV_STEPS = 2
HALO = 16
CHUNK = 1280
ROWS = 32
QUARTERS = 4
AXES = ("tm", "gz", "view")

RELAXATION = 0.9
STEP_SCALE = 0.3
STEP_DECAY = 0.7
SMOOTHING = 0.01
NORM_GUARD = 1e-06

F32 = jnp.float32
BF16 = jnp.bfloat16
WHOLE = pl.BlockSpec(memory_space=pltpu.VMEM)
SCALARS = pl.BlockSpec(memory_space=pltpu.SMEM)


def params(mib):
    return pltpu.CompilerParams(vmem_limit_bytes=mib * 1024 * 1024)


def near(array):
    return pltpu.with_memory_space_constraint(array, pltpu.VMEM)


def call(kernel, outs, ids, *arrays, scratch=()):
    return pl.pallas_call(
        kernel,
        out_shape=tuple(pltpu.VMEM(shape, dtype) for shape, dtype in outs),
        in_specs=[SCALARS] + [WHOLE] * len(arrays),
        out_specs=tuple(WHOLE for _ in outs),
        scratch_shapes=scratch,
        compiler_params=params(12),
    )(ids, *[near(a) for a in arrays])


def keeps(d):
    return d[4] == d[1] // 2


def move(array, rule, source=None):
    pairs = []
    for tm in range(2):
        for y in range(4):
            for h in range(2):
                for z in range(4):
                    for c in range(2):
                        here = (tm, y, h, z, c)
                        if source is not None and not source(here):
                            continue
                        there = rule(*here)
                        if there is None:
                            continue
                        index = [((t * 4 + a) * 2 + b) * 8 + 2 * u + v for t, a, b, u, v in (here, there)]
                        pairs.append(tuple(index))
    return lax.ppermute(array, AXES, pairs)


def after(array, *others):
    return lax.optimization_barrier((array, *others))[0]


def flip(dtm=0, dy=0, dh=0, dz=0, dc=0):
    return lambda tm, y, h, z, c: (tm ^ dtm, y ^ dy, h ^ dh, z ^ dz, c ^ dc)


def strip_step(step):
    def rule(tm, y, h, z, c):
        strip = 2 * tm + c + step
        return (strip // 2, y, h, z, strip % 2) if 0 <= strip < 4 else None

    return rule


def gram_kernel(ids_ref, a_ref, s0_ref, s1_ref, own_ref, send_ref, acc, level_ref):
    n = pl.program_id(0)
    rows, det = s0_ref.shape
    my_rows = pl.ds(pl.multiple_of(ids_ref[1] * rows, rows), rows)

    def chunk(d, first):
        at = pl.ds(d * CHUNK, CHUNK) if first else pl.ds(pl.multiple_of(d * CHUNK, CHUNK), CHUNK)
        tile = a_ref[:, at]
        ray = jnp.sum(tile.astype(F32), axis=0, keepdims=True)
        inverse = 1.0 / ray
        lhs = []
        for t, ref in enumerate((s0_ref, s1_ref)):
            scaled = ref[:, at].astype(F32) * inverse
            if first:
                mean = jnp.sum(scaled, axis=1, keepdims=True) / CHUNK
                level_ref[t] = jnp.broadcast_to(mean, level_ref.shape[1:])
            lhs.append((scaled - level_ref[t, :, 0:1]).astype(BF16))
        lhs.append((a_ref[my_rows, at].astype(F32) * inverse).astype(BF16))
        lhs.append(jnp.ones((16, CHUNK), BF16))
        stack = jnp.concatenate(lhs, axis=0)
        product = lax.dot_general(stack, tile, (((1,), (1,)), ((), ())), preferred_element_type=F32)
        if first:
            acc[...] = product
        else:
            acc[...] += product

    chunk(0, True)

    def further(d, carry):
        chunk(d, False)
        return carry

    lax.fori_loop(1, det // CHUNK, further, 0)

    part = rows // QUARTERS
    at = pl.ds(pl.multiple_of(n * part, part), part)
    for t in range(FRAMES):
        for ref, who in ((own_ref, 1 - t), (send_ref, t)):

            @pl.when(ids_ref[4] == who)
            def _():
                for quarter in range(QUARTERS):
                    lo = quarter * part
                    ref[jnp.bitwise_xor(ids_ref[2], quarter), at, :] = (
                        acc[t * rows + lo : t * rows + lo + part]
                        + level_ref[t, lo : lo + part, 0:1] * acc[3 * rows : 3 * rows + 1]
                    )

    for ref, mine_too in ((own_ref, True), (send_ref, False)):

        @pl.when((ids_ref[3] == n) == mine_too)
        def _():
            for quarter in range(QUARTERS):
                lo = 2 * rows + quarter * part
                ref[jnp.bitwise_xor(ids_ref[2], quarter), 2 * part : 3 * part, :] = acc[lo : lo + part]

        for half in range(2):

            @pl.when(n == half)
            def _():
                cover = acc[3 * rows : 3 * rows + 8]
                for k in range(QUARTERS):
                    ref[k, 3 * part + half : 3 * part + 8, :] = cover[half:8]


def gram_products(ids, projector, measured):
    _, pixels, det = projector.shape
    rows = measured.shape[2]
    part = rows // QUARTERS
    shape = (QUARTERS, 3 * part + 8, pixels)
    out = pl.BlockSpec(shape, lambda n, s: (0, 0, 0))
    projector = pltpu.with_memory_space_constraint(projector, pltpu.HBM)
    measured = pltpu.with_memory_space_constraint(measured, pltpu.HBM)
    return pl.pallas_call(
        gram_kernel,
        out_shape=(jax.ShapeDtypeStruct(shape, F32),) * 2,
        grid_spec=pltpu.PrefetchScalarGridSpec(
            num_scalar_prefetch=1,
            grid=(2,),
            in_specs=[
                pl.BlockSpec((None, pixels, det), lambda n, s: (s[8 + n], 0, 0)),
                pl.BlockSpec((None, None, rows, det), lambda n, s: (0, s[8 + n], 0, 0)),
                pl.BlockSpec((None, None, rows, det), lambda n, s: (1, s[8 + n], 0, 0)),
            ],
            out_specs=(out, out),
            scratch_shapes=[pltpu.VMEM((3 * rows + 16, pixels), F32), pltpu.VMEM((FRAMES, rows, RY), F32)],
        ),
        compiler_params=params(24),
        name="gram_products",
    )(ids, projector, measured, measured)


def chip_sum_kernel(ids_ref, own_ref, got_ref, *outs):
    for k, out in enumerate(outs):
        out[...] = own_ref[k] + got_ref[k]


def reduce_kernel(ids_ref, a0, a1, a2, a3, b_ref, gram_ref, aux_ref):
    part = gram_ref.shape[0]
    total = (a0[...] + a1[...]) + (a2[...] + a3[...])
    cov = total[3 * part : 3 * part + 8]
    scale = RELAXATION / cov
    share = cov / jnp.sum(cov, axis=1, keepdims=True)
    for n in range(2):
        b_ref[n] = total[n * part : (n + 1) * part] * scale[n : n + 1]
        aux_ref[n : n + 1] = RELAXATION * share[n : n + 1]
        aux_ref[2 + n : 3 + n] = scale[n : n + 1]
    rows = total[2 * part : 3 * part]
    own = jnp.sum(rows, axis=1, keepdims=True)
    mine = jnp.where(ids_ref[3] == 0, share[0:1], share[1:2])
    gram_ref[...] = (rows - own * mine).astype(BF16)


def place_gram_kernel(ids_ref, y0, y1, y2, y3, out_ref):
    z, y, h, tm = ids_ref[2], ids_ref[5], ids_ref[6], ids_ref[7]
    part = y0.shape[1]
    for dy, ref in enumerate((y0, y1, y2, y3)):
        for dx in range(4):
            slab = (
                jnp.bitwise_xor(tm, dx // 2) * 8
                + jnp.bitwise_xor(y, dy) * 2
                + jnp.bitwise_xor(h, dx % 2)
            )
            for k in range(QUARTERS):
                row = slab * (QUARTERS * part) + jnp.bitwise_xor(z, k) * part
                out_ref[pl.ds(pl.multiple_of(row, part), part), :] = ref[dx * QUARTERS + k]


def place_rows_kernel(ids_ref, z0, z1, z2, z3, out_ref, head_ref, tail_ref):
    z = ids_ref[2]
    part = z0.shape[2]
    for k, ref in enumerate((z0, z1, z2, z3)):
        start = jnp.bitwise_xor(z, k) * part
        for slab in range(4):
            for n in range(2):
                row = slab * (QUARTERS * part) + start
                out_ref[n, pl.ds(pl.multiple_of(row, part), part), :] = ref[slab, n]
    head_ref[...] = out_ref[:, :HALO]
    tail_ref[...] = out_ref[:, out_ref.shape[1] - HALO :]


def tv_into(x_ref, g_ref, ss_ref, flux_ref, first, depth):
    height, pixels = x_ref.shape
    blocks = pixels // RY

    @pl.when(first < 0)
    def _():
        x_ref[HALO - 1 : HALO, :] = x_ref[HALO : HALO + 1, :]

    @pl.when(first + height > depth)
    def _():
        x_ref[height - HALO : height - HALO + 1, :] = x_ref[height - HALO - 1 : height - HALO, :]

    column = (lax.broadcasted_iota(jnp.int32, (ROWS, RY), 1) < RY - 1).astype(F32)
    flux_ref[...] = jnp.zeros_like(flux_ref)

    def block(i, folded):
        here_at = pl.ds(pl.multiple_of(i * RY, RY), RY)
        next_at = pl.ds(pl.multiple_of(jnp.minimum(i + 1, blocks - 1) * RY, RY), RY)
        above = jnp.zeros((8, RY), F32)
        for lo in range(0, height, ROWS):
            hi = lo + ROWS
            here = x_ref[lo:hi, here_at]
            tail = x_ref[hi : hi + 8, here_at] if hi < height else here[ROWS - 8 :]
            below = pltpu.roll(jnp.concatenate([here, tail]), ROWS + 7, 0)[:ROWS]
            dz = below - here
            dc = (pltpu.roll(here, RY - 1, 1) - here) * column
            di = x_ref[lo:hi, next_at] - here
            square = dz * dz + dc * dc + di * di + SMOOTHING
            r = lax.rsqrt(square)
            r = r * (1.5 - (0.5 * square) * (r * r))
            fz = dz * r
            fc = dc * r
            fi = di * r
            over = pltpu.roll(jnp.concatenate([above, fz]), 1, 0)[8:]
            above = fz[ROWS - 8 :]
            g = (over - fz) + (flux_ref[lo:hi] - fi) + (pltpu.roll(fc, 1, 1) - fc)
            flux_ref[lo:hi] = fi
            g_ref[lo:hi, here_at] = g
            for k in range(0, ROWS, 8):
                if HALO <= lo + k < height - HALO:
                    folded = folded + g[k : k + 8] * g[k : k + 8]
        return folded

    ss_ref[...] = lax.fori_loop(0, blocks, block, jnp.zeros((8, RY), F32))


def descend(x_ref, g_ref, sums, step, cells):
    folded = (sums[0][...] + sums[1][...]) + (sums[2][...] + sums[3][...])
    total = jnp.sum(folded, axis=(0, 1), keepdims=True)
    factor = (STEP_SCALE * STEP_DECAY**step) / jnp.sqrt(total / cells + NORM_GUARD)
    return x_ref[...] - factor * g_ref[...]


def first_kernel(ids_ref, x_ref, x_out, g_ref, ss_ref, flux, *, depth):
    x_out[...] = x_ref[...]
    tv_into(x_out, g_ref, ss_ref, flux, ids_ref[0], depth)


def second_kernel(ids_ref, x_ref, g_ref, s0, s1, s2, s3, x_out, g_out, ss_out, flux, *, depth, step, cells):
    x_out[...] = descend(x_ref, g_ref, (s0, s1, s2, s3), step, cells)
    tv_into(x_out, g_out, ss_out, flux, ids_ref[0], depth)


def subset_kernel(
    ids_ref, x_ref, g_ref, s0, s1, s2, s3, mine_ref, other_ref, low_ref, b_ref, high_ref, aux_ref, *rest, depth, step, cells, last, final
):
    flux, product = rest[-2:]
    x_out = rest[0]
    height = x_ref.shape[0]
    parts = ((low_ref, 0, HALO), (b_ref, HALO, height - HALO), (high_ref, height - HALO, height))
    x_out[...] = descend(x_ref, g_ref, (s0, s1, s2, s3), step, cells)
    core = ids_ref[3]

    def subset(n, carry):
        rounded = x_out[...].astype(BF16)

        @pl.when(n == core)
        def _():
            product[...] = jnp.dot(rounded, mine_ref[...], preferred_element_type=F32)

        @pl.when(n != core)
        def _():
            product[...] = jnp.dot(rounded, other_ref[...], preferred_element_type=F32)

        along = jnp.sum(rounded.astype(F32) * aux_ref[pl.ds(n, 1), :], axis=1, keepdims=True)
        scale = aux_ref[pl.ds(2 + n, 1), :]
        for ref, lo, hi in parts:
            change = ref[n] - product[lo:hi] * scale - along[lo:hi]
            x_out[lo:hi] = jnp.maximum(x_out[lo:hi] + change, 0.0)
        return carry

    lax.fori_loop(0, 2, subset, 0)
    if last:
        slab_out = rest[1]
        rows = slab_out.shape[0]
        start = HALO + jnp.bitwise_and(ids_ref[1], 3) * rows
        slab_out[...] = x_out[pl.ds(pl.multiple_of(start, HALO), rows), :]
    if not final:
        g_out, ss_out = rest[1 + last : 3 + last]
        tv_into(x_out, g_out, ss_out, flux, ids_ref[0], depth)


def body(sinogram, projector, warm_volume, view_order):
    slices, pixels = warm_volume.shape
    part = slices // QUARTERS
    tm = lax.axis_index("tm").astype(jnp.int32)
    gz = lax.axis_index("gz").astype(jnp.int32)
    view = lax.axis_index("view").astype(jnp.int32)
    y, h = gz // 2, gz % 2
    z, c = view // 2, view % 2
    slab = tm * 8 + gz
    keeper = c == y // 2
    depth = slices * 16
    cells = depth * pixels
    inner = 4 * slices
    height = inner + 2 * HALO
    first = (2 * tm + c) * inner - HALO
    ids = jnp.stack([first, slab, z, c, keeper.astype(jnp.int32), y, h, tm])
    ids = jnp.concatenate([ids, view_order])

    def pair_of(unit):
        across = move(unit, flip(dh=1), keeps)
        return jnp.where(h == 0, jnp.stack([unit, across]), jnp.stack([across, unit]))

    def strip_of(pair):
        one, two, three = (move(pair, flip(dy=k), keeps) for k in range(1, 4))
        same = jnp.where(keeper, pair, two)
        flipped = jnp.where(keeper, one, three)
        return jnp.where(
            y % 2 == 0, jnp.concatenate([same, flipped]), jnp.concatenate([flipped, same])
        )

    def widen(array, dim):
        length = array.shape[dim]
        low = move(lax.slice_in_dim(array, length - HALO, length, axis=dim), strip_step(1))
        high = move(lax.slice_in_dim(array, 0, HALO, axis=dim), strip_step(-1))
        return jnp.concatenate([low, array, high], axis=dim)

    own, send = gram_products(ids, projector, sinogram)
    passed = move(send, flip(dc=1))
    warm_pair = pair_of(after(warm_volume, send))
    block = (own.shape[1:], F32)
    terms = call(chip_sum_kernel, [block] * QUARTERS, ids, own, passed)
    terms = [terms[0]] + [move(terms[k], flip(dz=k)) for k in range(1, QUARTERS)]
    b_unit, piece, aux = call(
        reduce_kernel,
        [((2, part, pixels), F32), ((part, pixels), BF16), ((8, pixels), F32)],
        ids,
        *terms,
    )

    line = jnp.stack([piece] + [move(piece, flip(dz=k)) for k in range(1, 4)])
    flips = (flip(dh=1), flip(dtm=1), flip(dtm=1, dh=1))
    plane = jnp.concatenate([line] + [move(line, f) for f in flips])
    spread = [move(plane, flip(dy=k)) for k in range(1, 4)]

    def along_z(strip):
        return [strip] + [move(strip, flip(dz=k)) for k in range(1, 4)]

    def b_rows(quarters):
        edge = ((2, HALO, pixels), F32)
        rows, head, tail = call(
            place_rows_kernel, [((2, inner, pixels), F32), edge, edge], ids, *quarters
        )
        return move(tail, strip_step(1)), rows, move(head, strip_step(-1))

    strip = strip_of(pair_of(b_unit))
    quarters = along_z(strip)

    big = ((height, pixels), F32)
    small = ((8, RY), F32)
    flux = pltpu.VMEM((height, RY), F32)

    def everyone(sums):
        flips = (flip(dc=1), flip(dtm=1), flip(dtm=1, dc=1))
        return [sums] + [move(sums, f) for f in flips]

    x = widen(strip_of(after(warm_pair, terms[0])).reshape(inner, pixels), 0)
    x = after(x, strip)
    x, g, sums = call(
        functools.partial(first_kernel, depth=depth), [big, big, small], ids, x, scratch=[flux]
    )
    b_wide = [None, None]
    finished = []
    for frame in range(FRAMES):
        for sweep in range(SWEEPS):
            step = sweep * TV_STEPS
            x, g, sums = call(
                functools.partial(second_kernel, depth=depth, step=step, cells=cells),
                [big, big, small],
                ids,
                x,
                g,
                *everyone(sums),
                scratch=[flux],
            )
            if frame == 0 and sweep == 0:
                (mine,) = call(
                    place_gram_kernel,
                    [((slices * 16, pixels), BF16)],
                    ids,
                    after(plane, sums),
                    *spread,
                )
                other = move(mine, flip(dc=1))
                b_wide[0] = b_rows(quarters)
                later = move(after(b_unit, sums), flip(dc=1), lambda d: not keeps(d))
                later = along_z(strip_of(pair_of(later)))
            if frame == 0 and sweep == 2:
                b_wide[1] = b_rows([after(later[0], x)] + later[1:])
            last = sweep == SWEEPS - 1
            final = last and frame == FRAMES - 1
            outs = [big] + [((slices, pixels), F32)] * last
            if not final:
                outs += [big, small]
            outs = call(
                functools.partial(
                    subset_kernel, depth=depth, step=step + 1, cells=cells, last=last, final=final
                ),
                outs,
                ids,
                x,
                g,
                *everyone(sums),
                mine,
                other,
                *b_wide[frame],
                aux,
                scratch=[flux, pltpu.VMEM((height, pixels), F32)],
            )
            x = outs[0]
            if not final:
                g, sums = outs[-2:]
        local = outs[1]
        passed = move(local, flip(dc=1), keeps)
        finished.append(jnp.where(keeper, local, passed))
    return jnp.stack(finished, axis=0)


def solution(mesh):
    return jax.shard_map(
        body,
        mesh=mesh,
        in_specs=(
            P(None, "view", ("tm", "gz"), None),
            P("view", None, None),
            P(("tm", "gz"), None),
            P(),
        ),
        out_specs=P(None, ("tm", "gz"), None),
        check_vma=False,
    )
```

```python
import functools

import jax
import jax.numpy as jnp
from jax import lax
from jax.experimental import pallas as pl
from jax.experimental.pallas import tpu as pltpu
from jax.sharding import PartitionSpec as P

RY = 128
FRAMES = 2
SWEEPS = 3
TV_STEPS = 2
HALO = 16
CHUNK = 1280
ROWS = 32
QUARTERS = 4
AXES = ("tm", "gz", "view")

RELAXATION = 0.9
STEP_SCALE = 0.3
STEP_DECAY = 0.7
SMOOTHING = 0.01
NORM_GUARD = 1e-06

F32 = jnp.float32
BF16 = jnp.bfloat16
WHOLE = pl.BlockSpec(memory_space=pltpu.VMEM)
SCALARS = pl.BlockSpec(memory_space=pltpu.SMEM)


def params(mib):
    return pltpu.CompilerParams(vmem_limit_bytes=mib * 1024 * 1024)


def near(array):
    return pltpu.with_memory_space_constraint(array, pltpu.VMEM)


def call(kernel, outs, ids, *arrays, scratch=()):
    return pl.pallas_call(
        kernel,
        out_shape=tuple(pltpu.VMEM(shape, dtype) for shape, dtype in outs),
        in_specs=[SCALARS] + [WHOLE] * len(arrays),
        out_specs=tuple(WHOLE for _ in outs),
        scratch_shapes=scratch,
        compiler_params=params(12),
    )(ids, *[near(a) for a in arrays])


def keeps(d):
    return d[4] == d[1] // 2


def move(array, rule, source=None):
    pairs = []
    for tm in range(2):
        for y in range(4):
            for h in range(2):
                for z in range(4):
                    for c in range(2):
                        here = (tm, y, h, z, c)
                        if source is not None and not source(here):
                            continue
                        there = rule(*here)
                        if there is None:
                            continue
                        index = [((t * 4 + a) * 2 + b) * 8 + 2 * u + v for t, a, b, u, v in (here, there)]
                        pairs.append(tuple(index))
    return lax.ppermute(array, AXES, pairs)


def after(array, *others):
    return lax.optimization_barrier((array, *others))[0]


def flip(dtm=0, dy=0, dh=0, dz=0, dc=0):
    return lambda tm, y, h, z, c: (tm ^ dtm, y ^ dy, h ^ dh, z ^ dz, c ^ dc)


def strip_step(step):
    def rule(tm, y, h, z, c):
        strip = 2 * tm + c + step
        return (strip // 2, y, h, z, strip % 2) if 0 <= strip < 4 else None

    return rule


def gram_kernel(ids_ref, a_ref, s0_ref, s1_ref, own_ref, send_ref, acc, level_ref):
    n = pl.program_id(0)
    rows, det = s0_ref.shape
    my_rows = pl.ds(pl.multiple_of(ids_ref[1] * rows, rows), rows)

    def chunk(d, first):
        at = pl.ds(d * CHUNK, CHUNK) if first else pl.ds(pl.multiple_of(d * CHUNK, CHUNK), CHUNK)
        tile = a_ref[:, at]
        ray = jnp.sum(tile.astype(F32), axis=0, keepdims=True)
        inverse = 1.0 / ray
        lhs = []
        for t, ref in enumerate((s0_ref, s1_ref)):
            scaled = ref[:, at].astype(F32) * inverse
            if first:
                mean = jnp.sum(scaled, axis=1, keepdims=True) / CHUNK
                level_ref[t] = jnp.broadcast_to(mean, level_ref.shape[1:])
            lhs.append((scaled - level_ref[t, :, 0:1]).astype(BF16))
        lhs.append((a_ref[my_rows, at].astype(F32) * inverse).astype(BF16))
        lhs.append(jnp.ones((16, CHUNK), BF16))
        stack = jnp.concatenate(lhs, axis=0)
        product = lax.dot_general(stack, tile, (((1,), (1,)), ((), ())), preferred_element_type=F32)
        if first:
            acc[...] = product
        else:
            acc[...] += product

    chunk(0, True)

    def further(d, carry):
        chunk(d, False)
        return carry

    lax.fori_loop(1, det // CHUNK, further, 0)

    part = rows // QUARTERS
    at = pl.ds(pl.multiple_of(n * part, part), part)
    for t in range(FRAMES):
        for ref, who in ((own_ref, 1 - t), (send_ref, t)):

            @pl.when(ids_ref[4] == who)
            def _():
                for quarter in range(QUARTERS):
                    lo = quarter * part
                    ref[jnp.bitwise_xor(ids_ref[2], quarter), at, :] = (
                        acc[t * rows + lo : t * rows + lo + part]
                        + level_ref[t, lo : lo + part, 0:1] * acc[3 * rows : 3 * rows + 1]
                    )

    for ref, mine_too in ((own_ref, True), (send_ref, False)):

        @pl.when((ids_ref[3] == n) == mine_too)
        def _():
            for quarter in range(QUARTERS):
                lo = 2 * rows + quarter * part
                ref[jnp.bitwise_xor(ids_ref[2], quarter), 2 * part : 3 * part, :] = acc[lo : lo + part]

        for half in range(2):

            @pl.when(n == half)
            def _():
                cover = acc[3 * rows : 3 * rows + 8]
                for k in range(QUARTERS):
                    ref[k, 3 * part + half : 3 * part + 8, :] = cover[half:8]


def gram_products(ids, projector, measured):
    _, pixels, det = projector.shape
    rows = measured.shape[2]
    part = rows // QUARTERS
    shape = (QUARTERS, 3 * part + 8, pixels)
    out = pl.BlockSpec(shape, lambda n, s: (0, 0, 0))
    projector = pltpu.with_memory_space_constraint(projector, pltpu.HBM)
    measured = pltpu.with_memory_space_constraint(measured, pltpu.HBM)
    return pl.pallas_call(
        gram_kernel,
        out_shape=(jax.ShapeDtypeStruct(shape, F32),) * 2,
        grid_spec=pltpu.PrefetchScalarGridSpec(
            num_scalar_prefetch=1,
            grid=(2,),
            in_specs=[
                pl.BlockSpec((None, pixels, det), lambda n, s: (s[8 + n], 0, 0)),
                pl.BlockSpec((None, None, rows, det), lambda n, s: (0, s[8 + n], 0, 0)),
                pl.BlockSpec((None, None, rows, det), lambda n, s: (1, s[8 + n], 0, 0)),
            ],
            out_specs=(out, out),
            scratch_shapes=[pltpu.VMEM((3 * rows + 16, pixels), F32), pltpu.VMEM((FRAMES, rows, RY), F32)],
        ),
        compiler_params=params(24),
        name="gram_products",
    )(ids, projector, measured, measured)


def chip_sum_kernel(ids_ref, own_ref, got_ref, *outs):
    for k, out in enumerate(outs):
        out[...] = own_ref[k] + got_ref[k]


def reduce_kernel(ids_ref, a0, a1, a2, a3, b_ref, gram_ref, aux_ref):
    part = gram_ref.shape[0]
    total = (a0[...] + a1[...]) + (a2[...] + a3[...])
    cov = total[3 * part : 3 * part + 8]
    scale = RELAXATION / cov
    share = cov / jnp.sum(cov, axis=1, keepdims=True)
    for n in range(2):
        b_ref[n] = total[n * part : (n + 1) * part] * scale[n : n + 1]
        aux_ref[n : n + 1] = RELAXATION * share[n : n + 1]
        aux_ref[2 + n : 3 + n] = scale[n : n + 1]
    rows = total[2 * part : 3 * part]
    own = jnp.sum(rows, axis=1, keepdims=True)
    mine = jnp.where(ids_ref[3] == 0, share[0:1], share[1:2])
    gram_ref[...] = (rows - own * mine).astype(BF16)


def place_gram_kernel(ids_ref, y0, y1, y2, y3, out_ref):
    z, y, h, tm = ids_ref[2], ids_ref[5], ids_ref[6], ids_ref[7]
    part = y0.shape[1]
    for dy, ref in enumerate((y0, y1, y2, y3)):
        for dx in range(4):
            slab = (
                jnp.bitwise_xor(tm, dx // 2) * 8
                + jnp.bitwise_xor(y, dy) * 2
                + jnp.bitwise_xor(h, dx % 2)
            )
            for k in range(QUARTERS):
                row = slab * (QUARTERS * part) + jnp.bitwise_xor(z, k) * part
                out_ref[pl.ds(pl.multiple_of(row, part), part), :] = ref[dx * QUARTERS + k]


def place_rows_kernel(ids_ref, z0, z1, z2, z3, out_ref, head_ref, tail_ref):
    z = ids_ref[2]
    part = z0.shape[2]
    for k, ref in enumerate((z0, z1, z2, z3)):
        start = jnp.bitwise_xor(z, k) * part
        for slab in range(4):
            for n in range(2):
                row = slab * (QUARTERS * part) + start
                out_ref[n, pl.ds(pl.multiple_of(row, part), part), :] = ref[slab, n]
    head_ref[...] = out_ref[:, :HALO]
    tail_ref[...] = out_ref[:, out_ref.shape[1] - HALO :]


def tv_into(x_ref, g_ref, ss_ref, flux_ref, first, depth):
    height, pixels = x_ref.shape
    blocks = pixels // RY

    @pl.when(first < 0)
    def _():
        x_ref[HALO - 1 : HALO, :] = x_ref[HALO : HALO + 1, :]

    @pl.when(first + height > depth)
    def _():
        x_ref[height - HALO : height - HALO + 1, :] = x_ref[height - HALO - 1 : height - HALO, :]

    column = (lax.broadcasted_iota(jnp.int32, (ROWS, RY), 1) < RY - 1).astype(F32)
    flux_ref[...] = jnp.zeros_like(flux_ref)

    def block(i, folded):
        here_at = pl.ds(pl.multiple_of(i * RY, RY), RY)
        next_at = pl.ds(pl.multiple_of(jnp.minimum(i + 1, blocks - 1) * RY, RY), RY)
        above = jnp.zeros((8, RY), F32)
        for lo in range(0, height, ROWS):
            hi = lo + ROWS
            here = x_ref[lo:hi, here_at]
            tail = x_ref[hi : hi + 8, here_at] if hi < height else here[ROWS - 8 :]
            below = pltpu.roll(jnp.concatenate([here, tail]), ROWS + 7, 0)[:ROWS]
            dz = below - here
            dc = (pltpu.roll(here, RY - 1, 1) - here) * column
            di = x_ref[lo:hi, next_at] - here
            square = dz * dz + dc * dc + di * di + SMOOTHING
            r = lax.rsqrt(square)
            r = r * (1.5 - (0.5 * square) * (r * r))
            fz = dz * r
            fc = dc * r
            fi = di * r
            over = pltpu.roll(jnp.concatenate([above, fz]), 1, 0)[8:]
            above = fz[ROWS - 8 :]
            g = (over - fz) + (flux_ref[lo:hi] - fi) + (pltpu.roll(fc, 1, 1) - fc)
            flux_ref[lo:hi] = fi
            g_ref[lo:hi, here_at] = g
            for k in range(0, ROWS, 8):
                if HALO <= lo + k < height - HALO:
                    folded = folded + g[k : k + 8] * g[k : k + 8]
        return folded

    ss_ref[...] = lax.fori_loop(0, blocks, block, jnp.zeros((8, RY), F32), unroll=2)


def descend(x_ref, g_ref, sums, step, cells):
    folded = (sums[0][...] + sums[1][...]) + (sums[2][...] + sums[3][...])
    total = jnp.sum(folded, axis=(0, 1), keepdims=True)
    factor = (STEP_SCALE * STEP_DECAY**step) / jnp.sqrt(total / cells + NORM_GUARD)
    return x_ref[...] - factor * g_ref[...]


def first_kernel(ids_ref, x_ref, x_out, g_ref, ss_ref, flux, *, depth):
    x_out[...] = x_ref[...]
    tv_into(x_out, g_ref, ss_ref, flux, ids_ref[0], depth)


def second_kernel(ids_ref, x_ref, g_ref, s0, s1, s2, s3, x_out, g_out, ss_out, flux, *, depth, step, cells):
    x_out[...] = descend(x_ref, g_ref, (s0, s1, s2, s3), step, cells)
    tv_into(x_out, g_out, ss_out, flux, ids_ref[0], depth)


def subset_kernel(
    ids_ref, x_ref, g_ref, s0, s1, s2, s3, mine_ref, other_ref, low_ref, b_ref, high_ref, aux_ref, *rest, depth, step, cells, last, final
):
    flux, product = rest[-2:]
    x_out = rest[0]
    height = x_ref.shape[0]
    parts = ((low_ref, 0, HALO), (b_ref, HALO, height - HALO), (high_ref, height - HALO, height))
    x_out[...] = descend(x_ref, g_ref, (s0, s1, s2, s3), step, cells)
    core = ids_ref[3]

    def subset(n, carry):
        rounded = x_out[...].astype(BF16)

        @pl.when(n == core)
        def _():
            product[...] = jnp.dot(rounded, mine_ref[...], preferred_element_type=F32)

        @pl.when(n != core)
        def _():
            product[...] = jnp.dot(rounded, other_ref[...], preferred_element_type=F32)

        along = jnp.sum(rounded.astype(F32) * aux_ref[pl.ds(n, 1), :], axis=1, keepdims=True)
        scale = aux_ref[pl.ds(2 + n, 1), :]
        for ref, lo, hi in parts:
            change = ref[n] - product[lo:hi] * scale - along[lo:hi]
            x_out[lo:hi] = jnp.maximum(x_out[lo:hi] + change, 0.0)
        return carry

    lax.fori_loop(0, 2, subset, 0)
    if last:
        slab_out = rest[1]
        rows = slab_out.shape[0]
        start = HALO + jnp.bitwise_and(ids_ref[1], 3) * rows
        slab_out[...] = x_out[pl.ds(pl.multiple_of(start, HALO), rows), :]
    if not final:
        g_out, ss_out = rest[1 + last : 3 + last]
        tv_into(x_out, g_out, ss_out, flux, ids_ref[0], depth)


def body(sinogram, projector, warm_volume, view_order):
    slices, pixels = warm_volume.shape
    part = slices // QUARTERS
    tm = lax.axis_index("tm").astype(jnp.int32)
    gz = lax.axis_index("gz").astype(jnp.int32)
    view = lax.axis_index("view").astype(jnp.int32)
    y, h = gz // 2, gz % 2
    z, c = view // 2, view % 2
    slab = tm * 8 + gz
    keeper = c == y // 2
    depth = slices * 16
    cells = depth * pixels
    inner = 4 * slices
    height = inner + 2 * HALO
    first = (2 * tm + c) * inner - HALO
    ids = jnp.stack([first, slab, z, c, keeper.astype(jnp.int32), y, h, tm])
    ids = jnp.concatenate([ids, view_order])

    def pair_of(unit):
        across = move(unit, flip(dh=1))
        return jnp.where(h == 0, jnp.stack([unit, across]), jnp.stack([across, unit]))

    def strip_of(pair):
        one, two, three = (move(pair, flip(dy=k), keeps) for k in range(1, 4))
        same = jnp.where(keeper, pair, two)
        flipped = jnp.where(keeper, one, three)
        return jnp.where(
            y % 2 == 0, jnp.concatenate([same, flipped]), jnp.concatenate([flipped, same])
        )

    def widen(array, dim):
        length = array.shape[dim]
        low = move(lax.slice_in_dim(array, length - HALO, length, axis=dim), strip_step(1))
        high = move(lax.slice_in_dim(array, 0, HALO, axis=dim), strip_step(-1))
        return jnp.concatenate([low, array, high], axis=dim)

    own, send = gram_products(ids, projector, sinogram)
    passed = move(send, flip(dc=1))
    warm_pair = pair_of(after(warm_volume, send))
    block = (own.shape[1:], F32)
    terms = call(chip_sum_kernel, [block] * QUARTERS, ids, own, passed)
    terms = [terms[0]] + [move(terms[k], flip(dz=k)) for k in range(1, QUARTERS)]
    b_unit, piece, aux = call(
        reduce_kernel,
        [((2, part, pixels), F32), ((part, pixels), BF16), ((8, pixels), F32)],
        ids,
        *terms,
    )

    line = jnp.stack([piece] + [move(piece, flip(dz=k)) for k in range(1, 4)])
    flips = (flip(dh=1), flip(dtm=1), flip(dtm=1, dh=1))
    plane = jnp.concatenate([line] + [move(line, f) for f in flips])
    spread = [move(plane, flip(dy=k)) for k in range(1, 4)]

    def along_z(strip):
        return [strip] + [move(strip, flip(dz=k)) for k in range(1, 4)]

    def b_rows(quarters):
        edge = ((2, HALO, pixels), F32)
        rows, head, tail = call(
            place_rows_kernel, [((2, inner, pixels), F32), edge, edge], ids, *quarters
        )
        return move(tail, strip_step(1)), rows, move(head, strip_step(-1))

    strip = strip_of(pair_of(b_unit))
    quarters = along_z(strip)
    later = move(after(b_unit, strip), flip(dc=1), lambda d: not keeps(d))
    later = along_z(strip_of(pair_of(later)))

    big = ((height, pixels), F32)
    small = ((8, RY), F32)
    flux = pltpu.VMEM((height, RY), F32)

    def everyone(sums):
        flips = (flip(dc=1), flip(dtm=1), flip(dtm=1, dc=1))
        return [sums] + [move(sums, f) for f in flips]

    x = widen(strip_of(after(warm_pair, terms[0])).reshape(inner, pixels), 0)
    x = after(x, strip)
    x, g, sums = call(
        functools.partial(first_kernel, depth=depth), [big, big, small], ids, x, scratch=[flux]
    )
    b_wide = [None, None]
    finished = []
    for frame in range(FRAMES):
        for sweep in range(SWEEPS):
            step = sweep * TV_STEPS
            x, g, sums = call(
                functools.partial(second_kernel, depth=depth, step=step, cells=cells),
                [big, big, small],
                ids,
                x,
                g,
                *everyone(sums),
                scratch=[flux],
            )
            if frame == 0 and sweep == 0:
                (mine,) = call(
                    place_gram_kernel,
                    [((slices * 16, pixels), BF16)],
                    ids,
                    after(plane, sums),
                    *spread,
                )
                other = move(mine, flip(dc=1))
                b_wide[0] = b_rows(quarters)
            if frame == 0 and sweep == 2:
                b_wide[1] = b_rows([after(later[0], x)] + later[1:])
            last = sweep == SWEEPS - 1
            final = last and frame == FRAMES - 1
            outs = [big] + [((slices, pixels), F32)] * last
            if not final:
                outs += [big, small]
            outs = call(
                functools.partial(
                    subset_kernel, depth=depth, step=step + 1, cells=cells, last=last, final=final
                ),
                outs,
                ids,
                x,
                g,
                *everyone(sums),
                mine,
                other,
                *b_wide[frame],
                aux,
                scratch=[flux, pltpu.VMEM((height, pixels), F32)],
            )
            x = outs[0]
            if not final:
                g, sums = outs[-2:]
        local = outs[1]
        passed = move(local, flip(dc=1), keeps)
        finished.append(jnp.where(keeper, local, passed))
    return jnp.stack(finished, axis=0)


def solution(mesh):
    return jax.shard_map(
        body,
        mesh=mesh,
        in_specs=(
            P(None, "view", ("tm", "gz"), None),
            P("view", None, None),
            P(("tm", "gz"), None),
            P(),
        ),
        out_specs=P(None, ("tm", "gz"), None),
        check_vma=False,
    )
```

```python
import functools

import jax
import jax.numpy as jnp
from jax import lax
from jax.experimental import pallas as pl
from jax.experimental.pallas import tpu as pltpu
from jax.sharding import PartitionSpec as P

RY = 128
FRAMES = 2
SWEEPS = 3
TV_STEPS = 2
HALO = 16
CHUNK = 1280
ROWS = 32
QUARTERS = 4
AXES = ("tm", "gz", "view")

RELAXATION = 0.9
STEP_SCALE = 0.3
STEP_DECAY = 0.7
SMOOTHING = 0.01
NORM_GUARD = 1e-06

F32 = jnp.float32
BF16 = jnp.bfloat16
WHOLE = pl.BlockSpec(memory_space=pltpu.VMEM)
SCALARS = pl.BlockSpec(memory_space=pltpu.SMEM)


def params(mib):
    return pltpu.CompilerParams(vmem_limit_bytes=mib * 1024 * 1024)


def near(array):
    return pltpu.with_memory_space_constraint(array, pltpu.VMEM)


def call(kernel, outs, ids, *arrays, scratch=()):
    return pl.pallas_call(
        kernel,
        out_shape=tuple(pltpu.VMEM(shape, dtype) for shape, dtype in outs),
        in_specs=[SCALARS] + [WHOLE] * len(arrays),
        out_specs=tuple(WHOLE for _ in outs),
        scratch_shapes=scratch,
        compiler_params=params(12),
    )(ids, *[near(a) for a in arrays])


def keeps(d):
    return d[4] == d[1] // 2


def move(array, rule, source=None):
    pairs = []
    for tm in range(2):
        for y in range(4):
            for h in range(2):
                for z in range(4):
                    for c in range(2):
                        here = (tm, y, h, z, c)
                        if source is not None and not source(here):
                            continue
                        there = rule(*here)
                        if there is None:
                            continue
                        index = [((t * 4 + a) * 2 + b) * 8 + 2 * u + v for t, a, b, u, v in (here, there)]
                        pairs.append(tuple(index))
    return lax.ppermute(array, AXES, pairs)


def after(array, *others):
    return lax.optimization_barrier((array, *others))[0]


def flip(dtm=0, dy=0, dh=0, dz=0, dc=0):
    return lambda tm, y, h, z, c: (tm ^ dtm, y ^ dy, h ^ dh, z ^ dz, c ^ dc)


def strip_step(step):
    def rule(tm, y, h, z, c):
        strip = 2 * tm + c + step
        return (strip // 2, y, h, z, strip % 2) if 0 <= strip < 4 else None

    return rule


def gram_kernel(ids_ref, a_ref, s0_ref, s1_ref, own_ref, send_ref, acc, level_ref):
    n = pl.program_id(0)
    rows, det = s0_ref.shape
    my_rows = pl.ds(pl.multiple_of(ids_ref[1] * rows, rows), rows)

    acc[...] = jnp.zeros_like(acc)

    def chunk(d, carry):
        at = pl.ds(pl.multiple_of(d * CHUNK, CHUNK), CHUNK)
        tile = a_ref[:, at]
        ray = jnp.sum(tile.astype(F32), axis=0, keepdims=True)
        inverse = 1.0 / ray
        lhs = []
        for t, ref in enumerate((s0_ref, s1_ref)):
            scaled = ref[:, at].astype(F32) * inverse

            @pl.when(d == 0)
            def _():
                mean = jnp.sum(scaled, axis=1, keepdims=True) / CHUNK
                level_ref[t] = jnp.broadcast_to(mean, level_ref.shape[1:])

            lhs.append((scaled - level_ref[t, :, 0:1]).astype(BF16))
        lhs.append((a_ref[my_rows, at].astype(F32) * inverse).astype(BF16))
        lhs.append(jnp.ones((16, CHUNK), BF16))
        stack = jnp.concatenate(lhs, axis=0)
        acc[...] += lax.dot_general(stack, tile, (((1,), (1,)), ((), ())), preferred_element_type=F32)
        return carry

    lax.fori_loop(0, det // CHUNK, chunk, 0)

    part = rows // QUARTERS
    at = pl.ds(pl.multiple_of(n * part, part), part)
    for t in range(FRAMES):
        for ref, who in ((own_ref, 1 - t), (send_ref, t)):

            @pl.when(ids_ref[4] == who)
            def _():
                for quarter in range(QUARTERS):
                    lo = quarter * part
                    ref[jnp.bitwise_xor(ids_ref[2], quarter), at, :] = (
                        acc[t * rows + lo : t * rows + lo + part]
                        + level_ref[t, lo : lo + part, 0:1] * acc[3 * rows : 3 * rows + 1]
                    )

    for ref, mine_too in ((own_ref, True), (send_ref, False)):

        @pl.when((ids_ref[3] == n) == mine_too)
        def _():
            for quarter in range(QUARTERS):
                lo = 2 * rows + quarter * part
                ref[jnp.bitwise_xor(ids_ref[2], quarter), 2 * part : 3 * part, :] = acc[lo : lo + part]

        for half in range(2):

            @pl.when(n == half)
            def _():
                cover = acc[3 * rows : 3 * rows + 8]
                for k in range(QUARTERS):
                    ref[k, 3 * part + half : 3 * part + 8, :] = cover[half:8]


def gram_products(ids, projector, measured):
    _, pixels, det = projector.shape
    rows = measured.shape[2]
    part = rows // QUARTERS
    shape = (QUARTERS, 3 * part + 8, pixels)
    out = pl.BlockSpec(shape, lambda n, s: (0, 0, 0))
    projector = pltpu.with_memory_space_constraint(projector, pltpu.HBM)
    measured = pltpu.with_memory_space_constraint(measured, pltpu.HBM)
    return pl.pallas_call(
        gram_kernel,
        out_shape=(jax.ShapeDtypeStruct(shape, F32),) * 2,
        grid_spec=pltpu.PrefetchScalarGridSpec(
            num_scalar_prefetch=1,
            grid=(2,),
            in_specs=[
                pl.BlockSpec((None, pixels, det), lambda n, s: (s[8 + n], 0, 0)),
                pl.BlockSpec((None, None, rows, det), lambda n, s: (0, s[8 + n], 0, 0)),
                pl.BlockSpec((None, None, rows, det), lambda n, s: (1, s[8 + n], 0, 0)),
            ],
            out_specs=(out, out),
            scratch_shapes=[pltpu.VMEM((3 * rows + 16, pixels), F32), pltpu.VMEM((FRAMES, rows, RY), F32)],
        ),
        compiler_params=params(24),
        name="gram_products",
    )(ids, projector, measured, measured)


def chip_sum_kernel(ids_ref, own_ref, got_ref, *outs):
    for k, out in enumerate(outs):
        out[...] = own_ref[k] + got_ref[k]


def reduce_kernel(ids_ref, a0, a1, a2, a3, b_ref, gram_ref, aux_ref):
    part = gram_ref.shape[0]
    total = (a0[...] + a1[...]) + (a2[...] + a3[...])
    cov = total[3 * part : 3 * part + 8]
    scale = RELAXATION / cov
    share = cov / jnp.sum(cov, axis=1, keepdims=True)
    for n in range(2):
        b_ref[n] = total[n * part : (n + 1) * part] * scale[n : n + 1]
        aux_ref[n : n + 1] = RELAXATION * share[n : n + 1]
        aux_ref[2 + n : 3 + n] = scale[n : n + 1]
    rows = total[2 * part : 3 * part]
    own = jnp.sum(rows, axis=1, keepdims=True)
    mine = jnp.where(ids_ref[3] == 0, share[0:1], share[1:2])
    gram_ref[...] = (rows - own * mine).astype(BF16)


def place_gram_kernel(ids_ref, y0, y1, y2, y3, out_ref):
    z, y, h, tm = ids_ref[2], ids_ref[5], ids_ref[6], ids_ref[7]
    part = y0.shape[1]
    for dy, ref in enumerate((y0, y1, y2, y3)):

        def place(dx, carry):
            slab = (
                jnp.bitwise_xor(tm, dx // 2) * 8
                + jnp.bitwise_xor(y, dy) * 2
                + jnp.bitwise_xor(h, dx % 2)
            )
            for k in range(QUARTERS):
                row = slab * (QUARTERS * part) + jnp.bitwise_xor(z, k) * part
                out_ref[pl.ds(pl.multiple_of(row, part), part), :] = ref[dx * QUARTERS + k]
            return carry

        lax.fori_loop(0, 4, place, 0)


def place_rows_kernel(ids_ref, z0, z1, z2, z3, out_ref, head_ref, tail_ref):
    z = ids_ref[2]
    part = z0.shape[2]
    for k, ref in enumerate((z0, z1, z2, z3)):
        start = jnp.bitwise_xor(z, k) * part

        def place(slab, carry):
            row = slab * (QUARTERS * part) + start
            for n in range(2):
                out_ref[n, pl.ds(pl.multiple_of(row, part), part), :] = ref[slab, n]
            return carry

        lax.fori_loop(0, 4, place, 0)
    head_ref[...] = out_ref[:, :HALO]
    tail_ref[...] = out_ref[:, out_ref.shape[1] - HALO :]


def tv_into(x_ref, g_ref, ss_ref, flux_ref, first, depth):
    height, pixels = x_ref.shape
    blocks = pixels // RY

    @pl.when(first < 0)
    def _():
        x_ref[HALO - 1 : HALO, :] = x_ref[HALO : HALO + 1, :]

    @pl.when(first + height > depth)
    def _():
        x_ref[height - HALO : height - HALO + 1, :] = x_ref[height - HALO - 1 : height - HALO, :]

    column = (lax.broadcasted_iota(jnp.int32, (ROWS, RY), 1) < RY - 1).astype(F32)
    flux_ref[...] = jnp.zeros_like(flux_ref)

    def block(i, folded):
        here_at = pl.ds(pl.multiple_of(i * RY, RY), RY)
        next_at = pl.ds(pl.multiple_of(jnp.minimum(i + 1, blocks - 1) * RY, RY), RY)
        above = jnp.zeros((8, RY), F32)
        for lo in range(0, height, ROWS):
            hi = lo + ROWS
            here = x_ref[lo:hi, here_at]
            tail = x_ref[hi : hi + 8, here_at] if hi < height else here[ROWS - 8 :]
            below = pltpu.roll(jnp.concatenate([here, tail]), ROWS + 7, 0)[:ROWS]
            dz = below - here
            dc = (pltpu.roll(here, RY - 1, 1) - here) * column
            di = x_ref[lo:hi, next_at] - here
            square = dz * dz + dc * dc + di * di + SMOOTHING
            r = lax.rsqrt(square)
            r = r * (1.5 - (0.5 * square) * (r * r))
            fz = dz * r
            fc = dc * r
            fi = di * r
            over = pltpu.roll(jnp.concatenate([above, fz]), 1, 0)[8:]
            above = fz[ROWS - 8 :]
            g = (over - fz) + (flux_ref[lo:hi] - fi) + (pltpu.roll(fc, 1, 1) - fc)
            flux_ref[lo:hi] = fi
            g_ref[lo:hi, here_at] = g
            for k in range(0, ROWS, 8):
                if HALO <= lo + k < height - HALO:
                    folded = folded + g[k : k + 8] * g[k : k + 8]
        return folded

    ss_ref[...] = lax.fori_loop(0, blocks, block, jnp.zeros((8, RY), F32), unroll=2)


def descend(x_ref, g_ref, sums, step, cells, x_out):
    folded = (sums[0][...] + sums[1][...]) + (sums[2][...] + sums[3][...])
    total = jnp.sum(folded, axis=(0, 1), keepdims=True)
    factor = (STEP_SCALE * STEP_DECAY**step) / jnp.sqrt(total / cells + NORM_GUARD)
    chunk = x_ref.shape[0] // 3

    def rows(k, carry):
        at = pl.ds(pl.multiple_of(k * chunk, 8), chunk)
        x_out[at, :] = x_ref[at, :] - factor * g_ref[at, :]
        return carry

    lax.fori_loop(0, 3, rows, 0)


def first_kernel(ids_ref, x_ref, x_out, g_ref, ss_ref, flux, *, depth):
    x_out[...] = x_ref[...]
    tv_into(x_out, g_ref, ss_ref, flux, ids_ref[0], depth)


def second_kernel(ids_ref, x_ref, g_ref, s0, s1, s2, s3, x_out, g_out, ss_out, flux, *, depth, step, cells):
    descend(x_ref, g_ref, (s0, s1, s2, s3), step, cells, x_out)
    tv_into(x_out, g_out, ss_out, flux, ids_ref[0], depth)


def subset_kernel(
    ids_ref, x_ref, g_ref, s0, s1, s2, s3, mine_ref, other_ref, low_ref, b_ref, high_ref, aux_ref, *rest, depth, step, cells, last, final
):
    flux, product = rest[-2:]
    x_out = rest[0]
    height = x_ref.shape[0]
    parts = ((low_ref, 0, HALO), (b_ref, HALO, height - HALO), (high_ref, height - HALO, height))
    descend(x_ref, g_ref, (s0, s1, s2, s3), step, cells, x_out)
    core = ids_ref[3]

    def subset(n, carry):
        rounded = x_out[...].astype(BF16)

        @pl.when(n == core)
        def _():
            product[...] = jnp.dot(rounded, mine_ref[...], preferred_element_type=F32)

        @pl.when(n != core)
        def _():
            product[...] = jnp.dot(rounded, other_ref[...], preferred_element_type=F32)

        along = jnp.sum(rounded.astype(F32) * aux_ref[pl.ds(n, 1), :], axis=1, keepdims=True)
        scale = aux_ref[pl.ds(2 + n, 1), :]
        for ref, lo, hi in parts:
            change = ref[n] - product[lo:hi] * scale - along[lo:hi]
            x_out[lo:hi] = jnp.maximum(x_out[lo:hi] + change, 0.0)
        return carry

    lax.fori_loop(0, 2, subset, 0)
    if last:
        slab_out = rest[1]
        rows = slab_out.shape[0]
        start = HALO + jnp.bitwise_and(ids_ref[1], 3) * rows
        slab_out[...] = x_out[pl.ds(pl.multiple_of(start, HALO), rows), :]
    if not final:
        g_out, ss_out = rest[1 + last : 3 + last]
        tv_into(x_out, g_out, ss_out, flux, ids_ref[0], depth)


def body(sinogram, projector, warm_volume, view_order):
    slices, pixels = warm_volume.shape
    part = slices // QUARTERS
    tm = lax.axis_index("tm").astype(jnp.int32)
    gz = lax.axis_index("gz").astype(jnp.int32)
    view = lax.axis_index("view").astype(jnp.int32)
    y, h = gz // 2, gz % 2
    z, c = view // 2, view % 2
    slab = tm * 8 + gz
    keeper = c == y // 2
    depth = slices * 16
    cells = depth * pixels
    inner = 4 * slices
    height = inner + 2 * HALO
    first = (2 * tm + c) * inner - HALO
    ids = jnp.stack([first, slab, z, c, keeper.astype(jnp.int32), y, h, tm])
    ids = jnp.concatenate([ids, view_order])

    def pair_of(unit):
        across = move(unit, flip(dh=1))
        return jnp.where(h == 0, jnp.stack([unit, across]), jnp.stack([across, unit]))

    def strip_of(pair):
        one, two, three = (move(pair, flip(dy=k), keeps) for k in range(1, 4))
        same = jnp.where(keeper, pair, two)
        flipped = jnp.where(keeper, one, three)
        return jnp.where(
            y % 2 == 0, jnp.concatenate([same, flipped]), jnp.concatenate([flipped, same])
        )

    def widen(array, dim):
        length = array.shape[dim]
        low = move(lax.slice_in_dim(array, length - HALO, length, axis=dim), strip_step(1))
        high = move(lax.slice_in_dim(array, 0, HALO, axis=dim), strip_step(-1))
        return jnp.concatenate([low, array, high], axis=dim)

    own, send = gram_products(ids, projector, sinogram)
    passed = move(send, flip(dc=1))
    warm_pair = pair_of(after(warm_volume, send))
    block = (own.shape[1:], F32)
    terms = call(chip_sum_kernel, [block] * QUARTERS, ids, own, passed)
    terms = [terms[0]] + [move(terms[k], flip(dz=k)) for k in range(1, QUARTERS)]
    b_unit, piece, aux = call(
        reduce_kernel,
        [((2, part, pixels), F32), ((part, pixels), BF16), ((8, pixels), F32)],
        ids,
        *terms,
    )

    line = jnp.stack([piece] + [move(piece, flip(dz=k)) for k in range(1, 4)])
    flips = (flip(dh=1), flip(dtm=1), flip(dtm=1, dh=1))
    plane = jnp.concatenate([line] + [move(line, f) for f in flips])
    spread = [move(plane, flip(dy=k)) for k in range(1, 4)]

    def along_z(strip):
        return [strip] + [move(strip, flip(dz=k)) for k in range(1, 4)]

    def b_rows(quarters):
        edge = ((2, HALO, pixels), F32)
        rows, head, tail = call(
            place_rows_kernel, [((2, inner, pixels), F32), edge, edge], ids, *quarters
        )
        return move(tail, strip_step(1)), rows, move(head, strip_step(-1))

    strip = strip_of(pair_of(b_unit))
    quarters = along_z(strip)
    later = move(after(b_unit, strip), flip(dc=1), lambda d: not keeps(d))
    later = along_z(strip_of(pair_of(later)))

    big = ((height, pixels), F32)
    small = ((8, RY), F32)
    flux = pltpu.VMEM((height, RY), F32)

    def everyone(sums):
        flips = (flip(dc=1), flip(dtm=1), flip(dtm=1, dc=1))
        return [sums] + [move(sums, f) for f in flips]

    x = widen(strip_of(after(warm_pair, terms[0])).reshape(inner, pixels), 0)
    x = after(x, strip)
    x, g, sums = call(
        functools.partial(first_kernel, depth=depth), [big, big, small], ids, x, scratch=[flux]
    )
    b_wide = [None, None]
    finished = []
    for frame in range(FRAMES):
        for sweep in range(SWEEPS):
            step = sweep * TV_STEPS
            x, g, sums = call(
                functools.partial(second_kernel, depth=depth, step=step, cells=cells),
                [big, big, small],
                ids,
                x,
                g,
                *everyone(sums),
                scratch=[flux],
            )
            if frame == 0 and sweep == 0:
                (mine,) = call(
                    place_gram_kernel,
                    [((slices * 16, pixels), BF16)],
                    ids,
                    after(plane, sums),
                    *spread,
                )
                other = move(mine, flip(dc=1))
                b_wide[0] = b_rows(quarters)
            if frame == 0 and sweep == 2:
                b_wide[1] = b_rows([after(later[0], x)] + later[1:])
            last = sweep == SWEEPS - 1
            final = last and frame == FRAMES - 1
            outs = [big] + [((slices, pixels), F32)] * last
            if not final:
                outs += [big, small]
            outs = call(
                functools.partial(
                    subset_kernel, depth=depth, step=step + 1, cells=cells, last=last, final=final
                ),
                outs,
                ids,
                x,
                g,
                *everyone(sums),
                mine,
                other,
                *b_wide[frame],
                aux,
                scratch=[flux, pltpu.VMEM((height, pixels), F32)],
            )
            x = outs[0]
            if not final:
                g, sums = outs[-2:]
        local = outs[1]
        passed = move(local, flip(dc=1), keeps)
        finished.append(jnp.where(keeper, local, passed))
    return jnp.stack(finished, axis=0)


def solution(mesh):
    return jax.shard_map(
        body,
        mesh=mesh,
        in_specs=(
            P(None, "view", ("tm", "gz"), None),
            P("view", None, None),
            P(("tm", "gz"), None),
            P(),
        ),
        out_specs=P(None, ("tm", "gz"), None),
        check_vma=False,
    )
```

```python
import functools

import jax
import jax.numpy as jnp
from jax import lax
from jax.experimental import pallas as pl
from jax.experimental.pallas import tpu as pltpu
from jax.sharding import PartitionSpec as P

RY = 128
FRAMES = 2
SWEEPS = 3
TV_STEPS = 2
HALO = 16
CHUNK = 1280
ROWS = 32
QUARTERS = 4
AXES = ("tm", "gz", "view")

RELAXATION = 0.9
STEP_SCALE = 0.3
STEP_DECAY = 0.7
SMOOTHING = 0.01
NORM_GUARD = 1e-06

F32 = jnp.float32
BF16 = jnp.bfloat16
WHOLE = pl.BlockSpec(memory_space=pltpu.VMEM)
SCALARS = pl.BlockSpec(memory_space=pltpu.SMEM)


def params(mib):
    return pltpu.CompilerParams(vmem_limit_bytes=mib * 1024 * 1024)


def near(array):
    return pltpu.with_memory_space_constraint(array, pltpu.VMEM)


def call(kernel, outs, ids, *arrays, scratch=()):
    return pl.pallas_call(
        kernel,
        out_shape=tuple(pltpu.VMEM(shape, dtype) for shape, dtype in outs),
        in_specs=[SCALARS] + [WHOLE] * len(arrays),
        out_specs=tuple(WHOLE for _ in outs),
        scratch_shapes=scratch,
        compiler_params=params(12),
    )(ids, *[near(a) for a in arrays])


def keeps(d):
    return d[4] == d[1] // 2


def move(array, rule, source=None):
    pairs = []
    for tm in range(2):
        for y in range(4):
            for h in range(2):
                for z in range(4):
                    for c in range(2):
                        here = (tm, y, h, z, c)
                        if source is not None and not source(here):
                            continue
                        there = rule(*here)
                        if there is None:
                            continue
                        index = [((t * 4 + a) * 2 + b) * 8 + 2 * u + v for t, a, b, u, v in (here, there)]
                        pairs.append(tuple(index))
    return lax.ppermute(array, AXES, pairs)


def after(array, *others):
    return lax.optimization_barrier((array, *others))[0]


def flip(dtm=0, dy=0, dh=0, dz=0, dc=0):
    return lambda tm, y, h, z, c: (tm ^ dtm, y ^ dy, h ^ dh, z ^ dz, c ^ dc)


def strip_step(step):
    def rule(tm, y, h, z, c):
        strip = 2 * tm + c + step
        return (strip // 2, y, h, z, strip % 2) if 0 <= strip < 4 else None

    return rule


def gram_kernel(ids_ref, a_ref, s0_ref, s1_ref, own_ref, send_ref, acc, level_ref):
    n = pl.program_id(0)
    rows, det = s0_ref.shape
    my_rows = pl.ds(pl.multiple_of(ids_ref[1] * rows, rows), rows)

    def chunk(d, first):
        at = pl.ds(d * CHUNK, CHUNK) if first else pl.ds(pl.multiple_of(d * CHUNK, CHUNK), CHUNK)
        tile = a_ref[:, at]
        ray = jnp.sum(tile.astype(F32), axis=0, keepdims=True)
        inverse = 1.0 / ray
        lhs = []
        for t, ref in enumerate((s0_ref, s1_ref)):
            scaled = ref[:, at].astype(F32) * inverse
            if first:
                mean = jnp.sum(scaled, axis=1, keepdims=True) / CHUNK
                level_ref[t] = jnp.broadcast_to(mean, level_ref.shape[1:])
            lhs.append((scaled - level_ref[t, :, 0:1]).astype(BF16))
        lhs.append((a_ref[my_rows, at].astype(F32) * inverse).astype(BF16))
        lhs.append(jnp.ones((16, CHUNK), BF16))
        stack = jnp.concatenate(lhs, axis=0)
        product = lax.dot_general(stack, tile, (((1,), (1,)), ((), ())), preferred_element_type=F32)
        if first:
            acc[...] = product
        else:
            acc[...] += product

    chunk(0, True)

    def further(d, carry):
        chunk(d, False)
        return carry

    lax.fori_loop(1, det // CHUNK, further, 0)

    part = rows // QUARTERS
    at = pl.ds(pl.multiple_of(n * part, part), part)
    for t in range(FRAMES):
        for ref, who in ((own_ref, 1 - t), (send_ref, t)):

            @pl.when(ids_ref[4] == who)
            def _():
                for quarter in range(QUARTERS):
                    lo = quarter * part
                    ref[jnp.bitwise_xor(ids_ref[2], quarter), at, :] = (
                        acc[t * rows + lo : t * rows + lo + part]
                        + level_ref[t, lo : lo + part, 0:1] * acc[3 * rows : 3 * rows + 1]
                    )

    for ref, mine_too in ((own_ref, True), (send_ref, False)):

        @pl.when((ids_ref[3] == n) == mine_too)
        def _():
            for quarter in range(QUARTERS):
                lo = 2 * rows + quarter * part
                ref[jnp.bitwise_xor(ids_ref[2], quarter), 2 * part : 3 * part, :] = acc[lo : lo + part]

        for half in range(2):

            @pl.when(n == half)
            def _():
                cover = acc[3 * rows : 3 * rows + 8]
                for k in range(QUARTERS):
                    ref[k, 3 * part + half : 3 * part + 8, :] = cover[half:8]


def gram_products(ids, projector, measured):
    _, pixels, det = projector.shape
    rows = measured.shape[2]
    part = rows // QUARTERS
    shape = (QUARTERS, 3 * part + 8, pixels)
    out = pl.BlockSpec(shape, lambda n, s: (0, 0, 0))
    projector = pltpu.with_memory_space_constraint(projector, pltpu.HBM)
    measured = pltpu.with_memory_space_constraint(measured, pltpu.HBM)
    return pl.pallas_call(
        gram_kernel,
        out_shape=(jax.ShapeDtypeStruct(shape, F32),) * 2,
        grid_spec=pltpu.PrefetchScalarGridSpec(
            num_scalar_prefetch=1,
            grid=(2,),
            in_specs=[
                pl.BlockSpec((None, pixels, det), lambda n, s: (s[8 + n], 0, 0)),
                pl.BlockSpec((None, None, rows, det), lambda n, s: (0, s[8 + n], 0, 0)),
                pl.BlockSpec((None, None, rows, det), lambda n, s: (1, s[8 + n], 0, 0)),
            ],
            out_specs=(out, out),
            scratch_shapes=[pltpu.VMEM((3 * rows + 16, pixels), F32), pltpu.VMEM((FRAMES, rows, RY), F32)],
        ),
        compiler_params=params(24),
        name="gram_products",
    )(ids, projector, measured, measured)


def chip_sum_kernel(ids_ref, own_ref, got_ref, *outs):
    for k, out in enumerate(outs):
        out[...] = own_ref[k] + got_ref[k]


def reduce_kernel(ids_ref, a0, a1, a2, a3, b_ref, gram_ref, aux_ref):
    part = gram_ref.shape[0]
    total = (a0[...] + a1[...]) + (a2[...] + a3[...])
    cov = total[3 * part : 3 * part + 8]
    scale = RELAXATION / cov
    share = cov / jnp.sum(cov, axis=1, keepdims=True)
    for n in range(2):
        b_ref[n] = total[n * part : (n + 1) * part] * scale[n : n + 1]
        aux_ref[n : n + 1] = RELAXATION * share[n : n + 1]
        aux_ref[2 + n : 3 + n] = scale[n : n + 1]
    rows = total[2 * part : 3 * part]
    own = jnp.sum(rows, axis=1, keepdims=True)
    mine = jnp.where(ids_ref[3] == 0, share[0:1], share[1:2])
    gram_ref[...] = (rows - own * mine).astype(BF16)


def place_gram_kernel(ids_ref, y0, y1, y2, y3, out_ref):
    z, y, h, tm = ids_ref[2], ids_ref[5], ids_ref[6], ids_ref[7]
    part = y0.shape[1]
    for dy, ref in enumerate((y0, y1, y2, y3)):

        def place(dx, carry):
            slab = (
                jnp.bitwise_xor(tm, dx // 2) * 8
                + jnp.bitwise_xor(y, dy) * 2
                + jnp.bitwise_xor(h, dx % 2)
            )
            for k in range(QUARTERS):
                row = slab * (QUARTERS * part) + jnp.bitwise_xor(z, k) * part
                out_ref[pl.ds(pl.multiple_of(row, part), part), :] = ref[dx * QUARTERS + k]
            return carry

        lax.fori_loop(0, 4, place, 0)


def place_rows_kernel(ids_ref, z0, z1, z2, z3, out_ref, head_ref, tail_ref):
    z = ids_ref[2]
    part = z0.shape[2]
    for k, ref in enumerate((z0, z1, z2, z3)):
        start = jnp.bitwise_xor(z, k) * part

        def place(slab, carry):
            row = slab * (QUARTERS * part) + start
            for n in range(2):
                out_ref[n, pl.ds(pl.multiple_of(row, part), part), :] = ref[slab, n]
            return carry

        lax.fori_loop(0, 4, place, 0)
    head_ref[...] = out_ref[:, :HALO]
    tail_ref[...] = out_ref[:, out_ref.shape[1] - HALO :]


def tv_into(x_ref, g_ref, ss_ref, flux_ref, first, depth):
    height, pixels = x_ref.shape
    blocks = pixels // RY

    @pl.when(first < 0)
    def _():
        x_ref[HALO - 1 : HALO, :] = x_ref[HALO : HALO + 1, :]

    @pl.when(first + height > depth)
    def _():
        x_ref[height - HALO : height - HALO + 1, :] = x_ref[height - HALO - 1 : height - HALO, :]

    column = (lax.broadcasted_iota(jnp.int32, (ROWS, RY), 1) < RY - 1).astype(F32)
    flux_ref[...] = jnp.zeros_like(flux_ref)

    def block(i, folded):
        here_at = pl.ds(pl.multiple_of(i * RY, RY), RY)
        next_at = pl.ds(pl.multiple_of(jnp.minimum(i + 1, blocks - 1) * RY, RY), RY)
        above = jnp.zeros((8, RY), F32)
        for lo in range(0, height, ROWS):
            hi = lo + ROWS
            here = x_ref[lo:hi, here_at]
            tail = x_ref[hi : hi + 8, here_at] if hi < height else here[ROWS - 8 :]
            below = pltpu.roll(jnp.concatenate([here, tail]), ROWS + 7, 0)[:ROWS]
            dz = below - here
            dc = (pltpu.roll(here, RY - 1, 1) - here) * column
            di = x_ref[lo:hi, next_at] - here
            square = dz * dz + dc * dc + di * di + SMOOTHING
            r = lax.rsqrt(square)
            r = r * (1.5 - (0.5 * square) * (r * r))
            fz = dz * r
            fc = dc * r
            fi = di * r
            over = pltpu.roll(jnp.concatenate([above, fz]), 1, 0)[8:]
            above = fz[ROWS - 8 :]
            g = (over - fz) + (flux_ref[lo:hi] - fi) + (pltpu.roll(fc, 1, 1) - fc)
            flux_ref[lo:hi] = fi
            g_ref[lo:hi, here_at] = g
            for k in range(0, ROWS, 8):
                if HALO <= lo + k < height - HALO:
                    folded = folded + g[k : k + 8] * g[k : k + 8]
        return folded

    ss_ref[...] = lax.fori_loop(0, blocks, block, jnp.zeros((8, RY), F32), unroll=2)


def descend(x_ref, g_ref, sums, step, cells, x_out):
    folded = (sums[0][...] + sums[1][...]) + (sums[2][...] + sums[3][...])
    total = jnp.sum(folded, axis=(0, 1), keepdims=True)
    factor = (STEP_SCALE * STEP_DECAY**step) / jnp.sqrt(total / cells + NORM_GUARD)
    chunk = x_ref.shape[0] // 3

    def rows(k, carry):
        at = pl.ds(pl.multiple_of(k * chunk, 8), chunk)
        x_out[at, :] = x_ref[at, :] - factor * g_ref[at, :]
        return carry

    lax.fori_loop(0, 3, rows, 0)


def first_kernel(ids_ref, x_ref, x_out, g_ref, ss_ref, flux, *, depth):
    x_out[...] = x_ref[...]
    tv_into(x_out, g_ref, ss_ref, flux, ids_ref[0], depth)


def second_kernel(ids_ref, x_ref, g_ref, s0, s1, s2, s3, x_out, g_out, ss_out, flux, *, depth, step, cells):
    descend(x_ref, g_ref, (s0, s1, s2, s3), step, cells, x_out)
    tv_into(x_out, g_out, ss_out, flux, ids_ref[0], depth)


def subset_kernel(
    ids_ref, x_ref, g_ref, s0, s1, s2, s3, mine_ref, other_ref, low_ref, b_ref, high_ref, aux_ref, *rest, depth, step, cells, last, final
):
    flux, product = rest[-2:]
    x_out = rest[0]
    height = x_ref.shape[0]
    parts = ((low_ref, 0, HALO), (b_ref, HALO, height - HALO), (high_ref, height - HALO, height))
    descend(x_ref, g_ref, (s0, s1, s2, s3), step, cells, x_out)
    core = ids_ref[3]

    def subset(n, carry):
        rounded = x_out[...].astype(BF16)

        @pl.when(n == core)
        def _():
            product[...] = jnp.dot(rounded, mine_ref[...], preferred_element_type=F32)

        @pl.when(n != core)
        def _():
            product[...] = jnp.dot(rounded, other_ref[...], preferred_element_type=F32)

        along = jnp.sum(rounded.astype(F32) * aux_ref[pl.ds(n, 1), :], axis=1, keepdims=True)
        scale = aux_ref[pl.ds(2 + n, 1), :]
        for ref, lo, hi in parts:
            change = ref[n] - product[lo:hi] * scale - along[lo:hi]
            x_out[lo:hi] = jnp.maximum(x_out[lo:hi] + change, 0.0)
        return carry

    lax.fori_loop(0, 2, subset, 0)
    if last:
        slab_out = rest[1]
        rows = slab_out.shape[0]
        start = HALO + jnp.bitwise_and(ids_ref[1], 3) * rows
        slab_out[...] = x_out[pl.ds(pl.multiple_of(start, HALO), rows), :]
    if not final:
        g_out, ss_out = rest[1 + last : 3 + last]
        tv_into(x_out, g_out, ss_out, flux, ids_ref[0], depth)


def body(sinogram, projector, warm_volume, view_order):
    slices, pixels = warm_volume.shape
    part = slices // QUARTERS
    tm = lax.axis_index("tm").astype(jnp.int32)
    gz = lax.axis_index("gz").astype(jnp.int32)
    view = lax.axis_index("view").astype(jnp.int32)
    y, h = gz // 2, gz % 2
    z, c = view // 2, view % 2
    slab = tm * 8 + gz
    keeper = c == y // 2
    depth = slices * 16
    cells = depth * pixels
    inner = 4 * slices
    height = inner + 2 * HALO
    first = (2 * tm + c) * inner - HALO
    ids = jnp.stack([first, slab, z, c, keeper.astype(jnp.int32), y, h, tm])
    ids = jnp.concatenate([ids, view_order])

    def pair_of(unit):
        across = move(unit, flip(dh=1))
        return jnp.where(h == 0, jnp.stack([unit, across]), jnp.stack([across, unit]))

    def strip_of(pair):
        one, two, three = (move(pair, flip(dy=k), keeps) for k in range(1, 4))
        same = jnp.where(keeper, pair, two)
        flipped = jnp.where(keeper, one, three)
        return jnp.where(
            y % 2 == 0, jnp.concatenate([same, flipped]), jnp.concatenate([flipped, same])
        )

    def widen(array, dim):
        length = array.shape[dim]
        low = move(lax.slice_in_dim(array, length - HALO, length, axis=dim), strip_step(1))
        high = move(lax.slice_in_dim(array, 0, HALO, axis=dim), strip_step(-1))
        return jnp.concatenate([low, array, high], axis=dim)

    own, send = gram_products(ids, projector, sinogram)
    passed = move(send, flip(dc=1))
    warm_pair = pair_of(after(warm_volume, send))
    block = (own.shape[1:], F32)
    terms = call(chip_sum_kernel, [block] * QUARTERS, ids, own, passed)
    terms = [terms[0]] + [move(terms[k], flip(dz=k)) for k in range(1, QUARTERS)]
    b_unit, piece, aux = call(
        reduce_kernel,
        [((2, part, pixels), F32), ((part, pixels), BF16), ((8, pixels), F32)],
        ids,
        *terms,
    )

    line = jnp.stack([piece] + [move(piece, flip(dz=k)) for k in range(1, 4)])
    flips = (flip(dh=1), flip(dtm=1), flip(dtm=1, dh=1))
    plane = jnp.concatenate([line] + [move(line, f) for f in flips])
    spread = [move(plane, flip(dy=k)) for k in range(1, 4)]

    def along_z(strip):
        return [strip] + [move(strip, flip(dz=k)) for k in range(1, 4)]

    def b_rows(quarters):
        edge = ((2, HALO, pixels), F32)
        rows, head, tail = call(
            place_rows_kernel, [((2, inner, pixels), F32), edge, edge], ids, *quarters
        )
        return move(tail, strip_step(1)), rows, move(head, strip_step(-1))

    strip = strip_of(pair_of(b_unit))
    quarters = along_z(strip)
    later = move(after(b_unit, strip), flip(dc=1), lambda d: not keeps(d))
    later = along_z(strip_of(pair_of(later)))

    big = ((height, pixels), F32)
    small = ((8, RY), F32)
    flux = pltpu.VMEM((height, RY), F32)

    def everyone(sums):
        flips = (flip(dc=1), flip(dtm=1), flip(dtm=1, dc=1))
        return [sums] + [move(sums, f) for f in flips]

    x = widen(strip_of(after(warm_pair, terms[0])).reshape(inner, pixels), 0)
    x = after(x, strip)
    x, g, sums = call(
        functools.partial(first_kernel, depth=depth), [big, big, small], ids, x, scratch=[flux]
    )
    b_wide = [None, None]
    finished = []
    for frame in range(FRAMES):
        for sweep in range(SWEEPS):
            step = sweep * TV_STEPS
            x, g, sums = call(
                functools.partial(second_kernel, depth=depth, step=step, cells=cells),
                [big, big, small],
                ids,
                x,
                g,
                *everyone(sums),
                scratch=[flux],
            )
            if frame == 0 and sweep == 0:
                (mine,) = call(
                    place_gram_kernel,
                    [((slices * 16, pixels), BF16)],
                    ids,
                    after(plane, sums),
                    *spread,
                )
                other = move(mine, flip(dc=1))
                b_wide[0] = b_rows(quarters)
            if frame == 0 and sweep == 2:
                b_wide[1] = b_rows([after(later[0], x)] + later[1:])
            last = sweep == SWEEPS - 1
            final = last and frame == FRAMES - 1
            outs = [big] + [((slices, pixels), F32)] * last
            if not final:
                outs += [big, small]
            outs = call(
                functools.partial(
                    subset_kernel, depth=depth, step=step + 1, cells=cells, last=last, final=final
                ),
                outs,
                ids,
                x,
                g,
                *everyone(sums),
                mine,
                other,
                *b_wide[frame],
                aux,
                scratch=[flux, pltpu.VMEM((height, pixels), F32)],
            )
            x = outs[0]
            if not final:
                g, sums = outs[-2:]
        local = outs[1]
        passed = move(local, flip(dc=1), keeps)
        finished.append(jnp.where(keeper, local, passed))
    return jnp.stack(finished, axis=0)


def solution(mesh):
    return jax.shard_map(
        body,
        mesh=mesh,
        in_specs=(
            P(None, "view", ("tm", "gz"), None),
            P("view", None, None),
            P(("tm", "gz"), None),
            P(),
        ),
        out_specs=P(None, ("tm", "gz"), None),
        check_vma=False,
    )
```
